32 devices in a mesh: grp: 2 (over y), stn: 8 (over z, x), tim: 2 (over core).
Axes of the slice: x: 2, y: 2, z: 4, core: 2. Of those that a mesh axis runs over, the one named last changes fastest.
Arguments:
- samples: bfloat16 [256, 32, 8192], P(('grp', 'stn'), 'tim'), parts along dimension 0, may hold values from -6 to 6
- taps: float32 [16, 8192], replicated, may hold values from -1.5 to 1.5
- flags: int32 [256, 32], P('grp'), parts along dimension 0, may hold values from 0 to 1, as said below
- group_owner: int32 [16], P('grp'), parts along dimension 0, may hold values from 0 to 7, each once
Outputs:
- visibility: float32 [16, 128, 2, 128], P(('grp', 'stn'), 'tim'), parts along dimension 0
The draws below stay inside these ranges and needn't reach their ends.
There are 2 independent parts, one for each index of `grp`. The reference program is written for one: setup_inputs(seed, part) draws one part's arguments, and reference() takes and returns one part's arrays. A program takes and returns all parts, laid end to end along the dimension named above; an argument that names none is the same for every part. Nothing has to cross between parts.
Inputs may be any that keep to these rules, and one draw needn't show every extreme that they name: `flags`: each channel's 1 entries form one circular run of consecutive frames, of length 0 to 32. `group_owner`: a permutation of the channel groups.
All inputs are finite; a program needn't handle non-finite values.
Results may differ from the reference program's by a relative error of at most 0.0063.
Values may be sent and summed in bfloat16 or wider, within the bound.
A program may use at most 320 MiB of HBM per device.

```python
import math
import jax
import jax.numpy as jnp
from jax import lax

INPUTS = 128
FFT = 8192
TAPS = 16
AVG = 16
BAND = 128
BAND_START = 1536
FRAMES = 32
N_STN = 8


def draw_flags(key, part):
    count_key, start_key = jax.random.split(jax.random.fold_in(key, 17))
    run_length = jax.random.randint(count_key, (BAND, 1), 0, FRAMES + 1)
    run_start = jax.random.randint(start_key, (BAND, 1), 0, FRAMES)
    positions = jnp.arange(FRAMES, dtype=jnp.int32)[None, :]
    return ((positions - run_start) % FRAMES < run_length).astype(jnp.int32)


def shard_levels(key, shape, cuts, least, top_value):
    loudness = 1.0
    for position, shards_of in cuts:
        steps = jax.random.uniform(jax.random.fold_in(jax.random.fold_in(key, 6), position), (shards_of,), jnp.float32, least / len(cuts), top_value / len(cuts))
        loudness = loudness * jnp.repeat(jnp.exp(steps), shape[position] // shards_of).reshape((-1,) + (1,) * (len(shape) - 1 - position))
    return loudness


def scatter_about(rng, dims, width, most, cuts=(), held_as=jnp.bfloat16):
    drawn = jax.random.normal(rng, dims, jnp.float32) * width
    if len(cuts) > 0:
        drawn = shard_levels(rng, dims, cuts, -0.22, 0.18) * drawn
    return jnp.clip(drawn, min=-most, max=most).astype(held_as)


def setup_inputs(seed: int = 0, part: int = 0) -> dict:
    key_of = jax.random.split(jax.random.key(seed), 5)
    own_keys = jax.random.split(jax.random.fold_in(key_of[4], part), 5)
    return {
        "samples": scatter_about(own_keys[0], (INPUTS, FRAMES, FFT), 1.0, 6.0, ((0, 8), (1, 2))),
        "taps": scatter_about(key_of[1], (TAPS, FFT), TAPS ** -0.5, 1.5, (), jnp.float32),
        "flags": draw_flags(jax.random.fold_in(jax.random.fold_in(key_of[4], part), 71), part),
        "group_owner": jax.random.permutation(own_keys[3], N_STN).astype(jnp.int32),
    }


def build_table(fft_len, channel_ids):
    positions = jnp.arange(fft_len, dtype=jnp.int32)
    phase_index = positions[:, None] * (BAND_START + channel_ids)[None, :] % fft_len
    angle = phase_index.astype(jnp.float32) * (2.0 * math.pi / fft_len)
    amplitude = 1.0 / math.sqrt(fft_len)
    real_part = jnp.cos(angle) * amplitude
    imag_part = -jnp.sin(angle) * amplitude
    return jnp.stack([real_part, imag_part], axis=-1).astype(jnp.bfloat16)

def reference(samples, taps, flags, group_owner):
    inputs, frames, fft_len = samples.shape
    band_width = flags.shape[0]
    group_total = band_width // AVG
    twiddle = build_table(fft_len, jnp.arange(band_width, dtype=jnp.int32)).astype(jnp.float32).reshape(fft_len, 2 * band_width)
    block_size = math.gcd(inputs, 64)

    def channelize(block_samples):
        padded = jnp.concatenate([jnp.zeros((block_size, TAPS - 1, fft_len), samples.dtype), block_samples], axis=1)
        filtered = jnp.zeros((block_size, frames, fft_len), jnp.float32)
        for tap_index in range(TAPS):
            filtered = filtered + taps[tap_index][None, None, :] * padded[:, tap_index:tap_index + frames, :].astype(jnp.float32)
        rounded = lax.optimization_barrier(filtered.astype(jnp.bfloat16))
        frame_rows = rounded.astype(jnp.float32).reshape(block_size * frames, fft_len)
        spectrum = jnp.dot(frame_rows, twiddle, precision=lax.Precision.HIGHEST).astype(jnp.bfloat16)
        return spectrum.reshape(block_size, frames, band_width, 2)
    spectra = lax.map(channelize, samples.reshape(inputs // block_size, block_size, frames, fft_len))
    spectra = spectra.reshape(inputs, frames, band_width, 2)
    weighted = spectra * flags.T.astype(jnp.bfloat16)[None, :, :, None]

    def correlate(group_id):
        sliced = lax.dynamic_slice_in_dim(weighted, group_id * AVG, AVG, axis=2).astype(jnp.float32)
        left_rows = sliced.reshape(inputs, -1)
        turned = jnp.stack([sliced[..., 1], -sliced[..., 0]], axis=-1).reshape(inputs, -1)
        real_part = jnp.dot(left_rows, left_rows.T, precision=lax.Precision.HIGHEST)
        imag_part = jnp.dot(turned, left_rows.T, precision=lax.Precision.HIGHEST)
        return jnp.stack([real_part, imag_part], axis=1) / (AVG * frames)
    owned_group = jnp.zeros((group_total,), jnp.int32).at[group_owner].set(jnp.arange(group_total, dtype=jnp.int32))
    return lax.map(correlate, owned_group)
```

```python
import functools
import math

import jax
import jax.numpy as jnp
import numpy as np
from jax import lax
from jax.experimental import pallas as pl
from jax.experimental.pallas import tpu as pltpu
from jax.sharding import PartitionSpec as P

BAND_START = 1536
MESH = pl.DeviceIdType.MESH
LANES = 128
ROW_BLOCK = 64
STEP_WIDTH = 1024
DEPTH = 256


def half_table(fft_len, channels):
    bins = np.arange(channels, dtype=np.int64) + BAND_START
    index = (np.arange(fft_len // 2, dtype=np.int64)[:, None] * bins[None]) % fft_len
    angle = index * (2.0 * math.pi / fft_len)
    amplitude = 1.0 / math.sqrt(fft_len)
    return np.cos(angle) * amplitude, -np.sin(angle) * amplitude


def table_constant(fft_len, groups, per_group):
    planes = [p.reshape(-1, groups, 1, per_group) for p in half_table(fft_len, groups * per_group)]
    stacked = np.concatenate(planes, axis=2)
    return stacked.reshape(stacked.shape[0], -1).astype(np.float32).astype(jnp.bfloat16)


def tree_sum(weights, frame, pairs):
    if len(pairs) == 1:
        return weights[pairs[0][0]] * frame[pairs[0][1]]
    middle = 1 << ((len(pairs) - 1).bit_length() - 1)
    return tree_sum(weights, frame, pairs[:middle]) + tree_sum(weights, frame, pairs[middle:])


def kernel(
    dims, owner_ref, samples_ref, taps_ref, table_ref, flags_ref, out_ref,
    wide, taps, table, flags, perm, turned_a, turned_b, rows_a, rows_b, totals, earlier,
    valid, spectra, outgoing, received, products, other,
    load_sem, taps_sem, table_sem, flags_sem, give_sem, take_sem, near_sem, send_sem, recv_sem, final_sem,
):
    stations, per_group = dims
    inputs, frames, fft_len = samples_ref.shape
    taps_count = taps_ref.shape[0]
    carry_rows = (taps_count - 1) * inputs
    own_rows = frames * inputs
    group_width = 2 * per_group
    columns = stations * group_width
    per_lane = LANES // group_width
    steps = fft_len // STEP_WIDTH
    half_steps = steps // 2
    chunks = STEP_WIDTH // LANES
    me = lax.axis_index("stn")
    half = lax.axis_index("tim")
    barrier = pltpu.get_barrier_semaphore()

    def stretch(j, base=0):
        return pl.ds(pl.multiple_of(base + j * STEP_WIDTH, STEP_WIDTH), STEP_WIDTH)

    def load(j):
        return pltpu.make_async_copy(
            samples_ref.at[:, :, stretch(j)], wide.at[:, :, stretch(j)], load_sem.at[j]
        )

    def load_taps(j):
        return pltpu.make_async_copy(taps_ref.at[:, stretch(j)], taps.at[:, stretch(j)], taps_sem.at[j])

    def load_table(j):
        return pltpu.make_async_copy(table_ref.at[stretch(j)], table.at[stretch(j)], table_sem.at[j])

    load_flags = pltpu.make_async_copy(flags_ref, flags, flags_sem.at[0])

    def give(j):
        return pltpu.make_async_remote_copy(
            src_ref=samples_ref.at[:, :, stretch(j, fft_len // 2)],
            dst_ref=wide.at[:, :, stretch(j, fft_len)],
            send_sem=give_sem.at[j],
            recv_sem=take_sem.at[j],
            device_id={"tim": 1 - half},
            device_id_type=MESH,
        )

    for j in range(steps):
        load(j).start()
        load_taps(j).start()
        if j < half_steps:
            load_table(j).start()
    load_flags.start()
    pl.semaphore_signal(barrier, inc=1, device_id={"tim": 1 - half}, device_id_type=MESH)

    def greet(d, carry):
        pl.semaphore_signal(
            barrier, inc=1, device_id={"stn": lax.rem(me + d, stations)}, device_id_type=MESH
        )
        return carry

    lax.fori_loop(1, stations, greet, 0)

    from_row = lax.broadcasted_iota(jnp.int32, (own_rows, own_rows), 0)
    from_column = lax.broadcasted_iota(jnp.int32, (own_rows, own_rows), 1)
    moving = (from_column == from_row % inputs * frames + from_row // inputs).astype(perm.dtype)
    for p in range(own_rows // LANES):
        perm[p] = moving[:, p * LANES : (p + 1) * LANES]

    def turn(offset, into):
        moving = jnp.concatenate([perm[p] for p in range(own_rows // LANES)], axis=1)
        for p in range(STEP_WIDTH // DEPTH):
            start = pl.multiple_of(offset + p * DEPTH, DEPTH)
            block = wide[:, :, pl.ds(start, DEPTH)].reshape(own_rows, DEPTH)
            moved = jnp.dot(moving, block, preferred_element_type=jnp.float32).astype(jnp.bfloat16)
            for q in range(DEPTH // LANES):
                into[p * (DEPTH // LANES) + q] = moved[:, q * LANES : (q + 1) * LANES]

    def filter_rows(j, base, turned, into, outputs):
        for c in range(chunks):
            lanes = pl.ds(pl.multiple_of(base + j * STEP_WIDTH + c * LANES, LANES), LANES)
            weights = [
                jnp.broadcast_to(taps[k : k + 1, lanes], (inputs, LANES)).astype(jnp.bfloat16)
                for k in range(taps_count)
            ]
            frame = [turned[c, s * inputs : (s + 1) * inputs, :] for s in range(frames)]
            for place, t in enumerate(outputs):
                first = t - (taps_count - 1)
                into[c, place * inputs : (place + 1) * inputs, :] = tree_sum(
                    weights, frame, [(k, first + k) for k in range(taps_count) if 0 <= first + k < frames]
                )

    def transform(rows, j, which, scale=None):
        stacked = jnp.concatenate([rows[c] for c in range(chunks)], axis=1)
        if columns <= DEPTH:
            totals[which] = add(totals[which], scale, stacked, table[stretch(j), :])
        else:

            def block(b, carry):
                to = pl.ds(pl.multiple_of(b * DEPTH, DEPTH), DEPTH)
                part = None if scale is None else scale[:, :DEPTH]
                totals[which, :, to] = add(totals[which, :, to], part, stacked, table[stretch(j), to])
                return carry

            lax.fori_loop(0, columns // DEPTH, block, 0)

    def add(held, scale, left, right):
        product = jnp.dot(left, right, preferred_element_type=jnp.float32)
        return held + product if scale is None else held * scale + product

    sign_row = lax.broadcasted_iota(jnp.int32, (1, columns), 1)
    bins = BAND_START + sign_row // group_width * per_group + sign_row % per_group
    sign = (1 - 2 * (bins % 2)).astype(jnp.float32)

    def sweep(count, trips, base, taps_base, outputs, total, other_total, follow, ready, flip, opening):
        def pair(i, carry):
            ready(i)
            even = 2 * i
            before = jnp.where(jnp.logical_and(opening, even == 0), 0, lax.rem(even + half_steps - 1, half_steps))
            scale = jnp.where(i == half_steps // 2, sign, 1.0) if flip else None
            turn(base + (even + 1) * STEP_WIDTH, turned_b)
            filter_rows(even, taps_base, turned_a, rows_a, outputs)
            transform(rows_b, before, jnp.where(i == 0, other_total, total))
            turn(jnp.where(even + 2 < count, base + (even + 2) * STEP_WIDTH, follow), turned_a)
            filter_rows(even + 1, taps_base, turned_b, rows_b, outputs)
            transform(rows_a, lax.rem(even, half_steps), total, scale)
            return carry

        lax.fori_loop(0, trips, pair, 0)

    def arrived(i):
        load(2 * i + 1).wait()

        @pl.when(2 * i + 2 < steps)
        def _():
            load(2 * i + 2).wait()

        for e in range(2):
            load_taps(2 * i + e).wait()

            @pl.when(i < half_steps // 2)
            def _():
                load_table(2 * i + e).wait()

    near = pltpu.make_async_remote_copy(
        src_ref=totals.at[1],
        dst_ref=earlier,
        send_sem=near_sem.at[0],
        recv_sem=near_sem.at[1],
        device_id={"tim": 1 - half},
        device_id_type=MESH,
    )
    own_outputs = range(frames)
    carry_outputs = range(frames, frames + taps_count - 1)
    totals[...] = jnp.zeros_like(totals)
    rows_b[...] = jnp.zeros_like(rows_b)
    load(0).wait()
    turn(0, turned_a)

    @pl.when(half == 0)
    def _():
        pl.semaphore_wait(barrier, stations)
        for j in range(half_steps):
            give(j).start()

    def own_ready(i):
        @pl.when(jnp.logical_or(half == 1, i >= half_steps // 2))
        def _():
            arrived(i)

        @pl.when(jnp.logical_and(half == 0, i == 1))
        def _():
            near.start()

        @pl.when(jnp.logical_and(half == 1, i == half_steps - 1))
        def _():
            give(0).wait_recv()

    def carry_ready(i):
        @pl.when(half == 0)
        def _():
            arrived(i)

        @pl.when(half == 1)
        def _():
            give(2 * i + 1).wait_recv()

            @pl.when(2 * i + 2 < half_steps)
            def _():
                give(2 * i + 2).wait_recv()

    def phase(p, carry):
        carrying = jnp.where(half == p, half_steps // 2, 0)
        owning = jnp.where(p == 0, half_steps, 0)
        sweep(
            half_steps, carrying, half * fft_len, half * (fft_len // 2), carry_outputs,
            1, 1 - half, 0, carry_ready, False, half == 0,
        )
        sweep(steps, owning, 0, 0, own_outputs, 0, 1 - half, half * fft_len, own_ready, True, half == 1)
        return carry

    lax.fori_loop(0, 2, phase, 0)
    transform(rows_b, half_steps - 1, half)

    @pl.when(half == 1)
    def _():
        pl.semaphore_wait(barrier, stations)

    load_flags.wait()
    band = stations * per_group
    channel = lax.broadcasted_iota(jnp.int32, (band, columns), 0)
    column = lax.broadcasted_iota(jnp.int32, (band, columns), 1)
    spread = (channel == column // group_width * per_group + column % per_group).astype(jnp.bfloat16)
    flag_rows = flags[...].astype(jnp.float32).astype(jnp.bfloat16)
    both = jnp.dot(flag_rows, spread, preferred_element_type=jnp.float32)
    valid[...] = jnp.where(half == 0, both[:frames], both[frames:])

    lane = lax.broadcasted_iota(jnp.int32, (8, columns), 1)
    target = lane % group_width
    for g in range(stations):
        target = jnp.where(lane // group_width == g, target + owner_ref[g] * group_width, target)
    target = target[:1]
    mask = valid[...].astype(jnp.bfloat16)

    def weigh(values, low, high):
        count = high - low
        shaped = values.astype(jnp.bfloat16).reshape(count, inputs, columns)
        spectra[low * inputs : high * inputs, :] = (shaped * mask[low:high, None, :]).reshape(
            count * inputs, columns
        )

    @pl.when(half == 0)
    def _():
        weigh(totals[0] * sign, 0, frames)

    @pl.when(half == 1)
    def _():
        near.wait_recv()
        carried = carry_rows // inputs
        weigh((totals[0, :carry_rows, :] + totals[1, :carry_rows, :]) * sign + earlier[:carry_rows, :], 0, carried)
        weigh(totals[0, carry_rows:, :] * sign, carried, frames)

    slot = lax.broadcasted_iota(jnp.int32, (inputs, LANES), 1) // group_width

    def turn_copy(d):
        to = lax.rem(me + d, stations)
        return pltpu.make_async_remote_copy(
            src_ref=outgoing.at[to],
            dst_ref=received.at[me],
            send_sem=send_sem.at[d],
            recv_sem=recv_sem.at[d],
            device_id={"stn": to},
            device_id_type=MESH,
        )

    def arrange(order, carry):
        b = lax.rem(order + 1 + me // per_lane, stations // per_lane)
        row = lax.broadcasted_iota(jnp.int32, (LANES, columns), 0) + b * LANES
        picked = (row == target).astype(jnp.bfloat16)
        block = lax.dot_general(
            spectra[...], picked, (((1,), (1,)), ((), ())), preferred_element_type=jnp.float32
        )
        for r in range(per_lane):
            for quad in range(frames // per_lane):
                joined = jnp.zeros((inputs, LANES), jnp.float32)
                for t in range(per_lane):
                    first = (quad * per_lane + t) * inputs
                    piece = block[first : first + inputs, :]
                    if t != r:
                        piece = pltpu.roll(piece, ((t - r) * group_width) % LANES, 1)
                    joined = jnp.where(slot == t, piece, joined)
                outgoing[b * per_lane + r, :, quad * LANES : (quad + 1) * LANES] = joined.astype(
                    jnp.bfloat16
                )
        for r in range(per_lane):
            to = b * per_lane + r

            @pl.when(to != me)
            def _():
                turn_copy(lax.rem(to - me + stations, stations)).start()

        return carry

    lax.fori_loop(0, stations // per_lane, arrange, 0)

    received[me] = outgoing[me]

    def arrive(d, carry):
        turn_copy(d).wait_recv()
        return carry

    lax.fori_loop(1, stations, arrive, 0)

    total_inputs = stations * inputs
    length = frames * group_width
    per_block = ROW_BLOCK // inputs
    plane = lax.broadcasted_iota(jnp.int32, (ROW_BLOCK, length), 1) // per_group % 2
    everything = received[...].reshape(total_inputs, length)

    def correlate(b, carry):
        left = received[pl.ds(b * per_block, per_block)].reshape(ROW_BLOCK, length)
        full = left.astype(jnp.float32)
        turned = jnp.where(
            plane == 0, pltpu.roll(full, length - per_group, 1), -pltpu.roll(full, per_group, 1)
        ).astype(jnp.bfloat16)
        pair = jnp.concatenate([left, turned], axis=0)
        product = lax.dot_general(
            pair, everything, (((1,), (1,)), ((), ())), preferred_element_type=jnp.float32
        )
        products[b] = product.reshape(2, ROW_BLOCK, total_inputs)
        return carry

    blocks = out_ref.shape[0]
    last = pltpu.make_async_remote_copy(
        src_ref=products.at[pl.ds((1 - half) * blocks, blocks)],
        dst_ref=other,
        send_sem=final_sem.at[0],
        recv_sem=final_sem.at[1],
        device_id={"tim": 1 - half},
        device_id_type=MESH,
    )
    lax.fori_loop((1 - half) * blocks, (2 - half) * blocks, correlate, 0)
    last.start()
    lax.fori_loop(half * blocks, (1 + half) * blocks, correlate, 0)

    def sent(d, carry):
        turn_copy(d).wait_send()
        return carry

    lax.fori_loop(1, stations, sent, 0)

    @pl.when(half == 0)
    def _():
        near.wait_send()
        for j in range(half_steps):
            give(j).wait_send()

    last.wait()
    normaliser = 1.0 / (per_group * frames * 2)
    out_ref[...] = (products[pl.ds(half * blocks, blocks)] + other[...]) * normaliser


def per_device(samples, taps, flags, group_owner):
    inputs, frames, fft_len = samples.shape
    taps_count = taps.shape[0]
    stations = lax.axis_size("stn")
    band = flags.shape[0]
    per_group = band // stations
    columns = 2 * band
    total_inputs = stations * inputs
    blocks = total_inputs // ROW_BLOCK
    length = frames * 2 * per_group
    steps = fft_len // STEP_WIDTH
    chunks = STEP_WIDTH // LANES
    own_rows = frames * inputs
    table = jnp.asarray(table_constant(fft_len, stations, per_group))
    hbm = pl.BlockSpec(memory_space=pltpu.HBM)
    result = pl.pallas_call(
        functools.partial(kernel, (stations, per_group)),
        in_specs=[pl.BlockSpec(memory_space=pltpu.SMEM), hbm, hbm, hbm, hbm],
        out_specs=pl.BlockSpec(memory_space=pltpu.VMEM),
        out_shape=jax.ShapeDtypeStruct((blocks // 2, 2, ROW_BLOCK, total_inputs), jnp.float32),
        scratch_shapes=[
            pltpu.VMEM((inputs, frames, fft_len + fft_len // 2), jnp.bfloat16),
            pltpu.VMEM((taps_count, fft_len), jnp.float32),
            pltpu.VMEM((fft_len // 2, columns), jnp.bfloat16),
            pltpu.VMEM((flags.shape[1], band), jnp.int32),
            pltpu.VMEM((own_rows // LANES, own_rows, LANES), jnp.bfloat16),
            pltpu.VMEM((chunks, own_rows, LANES), jnp.bfloat16),
            pltpu.VMEM((chunks, own_rows, LANES), jnp.bfloat16),
            pltpu.VMEM((chunks, own_rows, LANES), jnp.bfloat16),
            pltpu.VMEM((chunks, own_rows, LANES), jnp.bfloat16),
            pltpu.VMEM((2, own_rows, columns), jnp.float32),
            pltpu.VMEM((own_rows, columns), jnp.float32),
            pltpu.VMEM((frames, columns), jnp.float32),
            pltpu.VMEM((own_rows, columns), jnp.bfloat16),
            pltpu.VMEM((stations, inputs, length), jnp.bfloat16),
            pltpu.VMEM((stations, inputs, length), jnp.bfloat16),
            pltpu.VMEM((blocks, 2, ROW_BLOCK, total_inputs), jnp.float32),
            pltpu.VMEM((blocks // 2, 2, ROW_BLOCK, total_inputs), jnp.float32),
            pltpu.SemaphoreType.DMA((steps,)),
            pltpu.SemaphoreType.DMA((steps,)),
            pltpu.SemaphoreType.DMA((steps // 2,)),
            pltpu.SemaphoreType.DMA((1,)),
            pltpu.SemaphoreType.DMA((steps // 2,)),
            pltpu.SemaphoreType.DMA((steps // 2,)),
            pltpu.SemaphoreType.DMA((2,)),
            pltpu.SemaphoreType.DMA((stations,)),
            pltpu.SemaphoreType.DMA((stations,)),
            pltpu.SemaphoreType.DMA((2,)),
        ],
        compiler_params=pltpu.CompilerParams(
            collective_id=0, has_side_effects=True, vmem_limit_bytes=60 << 20
        ),
        name="correlator",
    )(group_owner, samples, taps, table, flags.T)
    return result.transpose(0, 2, 1, 3).reshape(1, -1, 2, total_inputs)


def solution(mesh):
    in_specs = (P(("grp", "stn"), "tim", None), P(), P("grp", None), P("grp"))
    out_specs = P(("grp", "stn"), "tim", None, None)
    return jax.shard_map(
        per_device, mesh=mesh, in_specs=in_specs, out_specs=out_specs, check_vma=False
    )
```

```python
import functools
import math

import jax
import jax.numpy as jnp
import numpy as np
from jax import lax
from jax.experimental import pallas as pl
from jax.experimental.pallas import tpu as pltpu
from jax.sharding import PartitionSpec as P

BAND_START = 1536
MESH = pl.DeviceIdType.MESH
LANES = 128
ROW_BLOCK = 64
STEP_WIDTH = 1024
DEPTH = 256
KEPT_LIMIT = 1 << 20


def half_table(fft_len, channels):
    bins = np.arange(channels, dtype=np.int64) + BAND_START
    index = (np.arange(fft_len // 2, dtype=np.int64)[:, None] * bins[None]) % fft_len
    angle = index * (2.0 * math.pi / fft_len)
    amplitude = 1.0 / math.sqrt(fft_len)
    return np.cos(angle) * amplitude, -np.sin(angle) * amplitude


def table_constant(fft_len, groups, per_group):
    planes = [p.reshape(-1, groups, 1, per_group) for p in half_table(fft_len, groups * per_group)]
    stacked = np.concatenate(planes, axis=2)
    return stacked.reshape(stacked.shape[0], -1).astype(np.float32).astype(jnp.bfloat16)


def tree_sum(weights, frame, pairs):
    if len(pairs) == 1:
        return weights[pairs[0][0]] * frame[pairs[0][1]]
    middle = 1 << ((len(pairs) - 1).bit_length() - 1)
    return tree_sum(weights, frame, pairs[:middle]) + tree_sum(weights, frame, pairs[middle:])


def kernel(
    dims, owner_ref, samples_ref, taps_ref, table_ref, flags_ref, out_ref,
    wide, taps, table, flags, perm, turned_a, turned_b, rows_a, rows_b, totals, earlier,
    valid, spectra, outgoing, received, products, other,
    load_sem, taps_sem, table_sem, flags_sem, give_sem, take_sem, near_sem, send_sem, recv_sem, final_sem,
):
    stations, per_group = dims
    inputs, frames, fft_len = samples_ref.shape
    taps_count = taps_ref.shape[0]
    carry_rows = (taps_count - 1) * inputs
    own_rows = frames * inputs
    group_width = 2 * per_group
    columns = stations * group_width
    per_lane = LANES // group_width
    steps = fft_len // STEP_WIDTH
    half_steps = steps // 2
    chunks = STEP_WIDTH // LANES
    me = lax.axis_index("stn")
    half = lax.axis_index("tim")
    barrier = pltpu.get_barrier_semaphore()

    def stretch(j, base=0):
        return pl.ds(pl.multiple_of(base + j * STEP_WIDTH, STEP_WIDTH), STEP_WIDTH)

    def load(j):
        return pltpu.make_async_copy(
            samples_ref.at[:, :, stretch(j)], wide.at[:, :, stretch(j)], load_sem.at[j]
        )

    def load_taps(j):
        return pltpu.make_async_copy(taps_ref.at[:, stretch(j)], taps.at[:, stretch(j)], taps_sem.at[j])

    def load_table(j):
        return pltpu.make_async_copy(table_ref.at[stretch(j)], table.at[stretch(j)], table_sem.at[j])

    load_flags = pltpu.make_async_copy(flags_ref, flags, flags_sem.at[0])

    def give(j):
        return pltpu.make_async_remote_copy(
            src_ref=samples_ref.at[:, :, stretch(j, fft_len // 2)],
            dst_ref=wide.at[:, :, stretch(j, fft_len)],
            send_sem=give_sem.at[j],
            recv_sem=take_sem.at[j],
            device_id={"tim": 1 - half},
            device_id_type=MESH,
        )

    for j in range(steps):
        load(j).start()
        load_taps(j).start()
        if j < half_steps:
            load_table(j).start()
    load_flags.start()
    pl.semaphore_signal(barrier, inc=1, device_id={"tim": 1 - half}, device_id_type=MESH)

    def greet(d, carry):
        pl.semaphore_signal(
            barrier, inc=1, device_id={"stn": lax.rem(me + d, stations)}, device_id_type=MESH
        )
        return carry

    lax.fori_loop(1, stations, greet, 0)

    from_row = lax.broadcasted_iota(jnp.int32, (own_rows, own_rows), 0)
    from_column = lax.broadcasted_iota(jnp.int32, (own_rows, own_rows), 1)
    moving = (from_column == from_row % inputs * frames + from_row // inputs).astype(perm.dtype)
    for p in range(own_rows // LANES):
        perm[p] = moving[:, p * LANES : (p + 1) * LANES]

    def turn(offset, into):
        moving = jnp.concatenate([perm[p] for p in range(own_rows // LANES)], axis=1)
        for p in range(STEP_WIDTH // DEPTH):
            start = pl.multiple_of(offset + p * DEPTH, DEPTH)
            block = wide[:, :, pl.ds(start, DEPTH)].reshape(own_rows, DEPTH)
            moved = jnp.dot(moving, block, preferred_element_type=jnp.float32).astype(jnp.bfloat16)
            for q in range(DEPTH // LANES):
                into[p * (DEPTH // LANES) + q] = moved[:, q * LANES : (q + 1) * LANES]

    def filter_rows(j, base, turned, into, outputs):
        for c in range(chunks):
            lanes = pl.ds(pl.multiple_of(base + j * STEP_WIDTH + c * LANES, LANES), LANES)
            weights = [
                jnp.broadcast_to(taps[k : k + 1, lanes], (inputs, LANES)).astype(jnp.bfloat16)
                for k in range(taps_count)
            ]
            frame = [turned[c, s * inputs : (s + 1) * inputs, :] for s in range(frames)]
            for place, t in enumerate(outputs):
                first = t - (taps_count - 1)
                into[c, place * inputs : (place + 1) * inputs, :] = tree_sum(
                    weights, frame, [(k, first + k) for k in range(taps_count) if 0 <= first + k < frames]
                )

    def transform(rows, j, which, scale=None):
        stacked = jnp.concatenate([rows[c] for c in range(chunks)], axis=1)
        if columns <= DEPTH:
            totals[which] = add(totals[which], scale, stacked, table[stretch(j), :])
        else:

            def block(b, carry):
                to = pl.ds(pl.multiple_of(b * DEPTH, DEPTH), DEPTH)
                part = None if scale is None else scale[:, :DEPTH]
                totals[which, :, to] = add(totals[which, :, to], part, stacked, table[stretch(j), to])
                return carry

            lax.fori_loop(0, columns // DEPTH, block, 0)

    def add(held, scale, left, right):
        product = jnp.dot(left, right, preferred_element_type=jnp.float32)
        return held + product if scale is None else held * scale + product

    sign_row = lax.broadcasted_iota(jnp.int32, (1, columns), 1)
    bins = BAND_START + sign_row // group_width * per_group + sign_row % per_group
    sign = (1 - 2 * (bins % 2)).astype(jnp.float32)

    def sweep(count, trips, base, taps_base, outputs, total, other_total, follow, ready, flip, opening):
        def pair(i, carry):
            ready(i)
            even = 2 * i
            before = jnp.where(jnp.logical_and(opening, even == 0), 0, lax.rem(even + half_steps - 1, half_steps))
            scale = jnp.where(i == half_steps // 2, sign, 1.0) if flip else None
            turn(base + (even + 1) * STEP_WIDTH, turned_b)
            filter_rows(even, taps_base, turned_a, rows_a, outputs)
            transform(rows_b, before, jnp.where(i == 0, other_total, total))
            turn(jnp.where(even + 2 < count, base + (even + 2) * STEP_WIDTH, follow), turned_a)
            filter_rows(even + 1, taps_base, turned_b, rows_b, outputs)
            transform(rows_a, lax.rem(even, half_steps), total, scale)
            return carry

        lax.fori_loop(0, trips, pair, 0)

    def arrived(i):
        load(2 * i + 1).wait()

        @pl.when(2 * i + 2 < steps)
        def _():
            load(2 * i + 2).wait()

        for e in range(2):
            load_taps(2 * i + e).wait()

            @pl.when(i < half_steps // 2)
            def _():
                load_table(2 * i + e).wait()

    near = pltpu.make_async_remote_copy(
        src_ref=totals.at[1],
        dst_ref=earlier,
        send_sem=near_sem.at[0],
        recv_sem=near_sem.at[1],
        device_id={"tim": 1 - half},
        device_id_type=MESH,
    )
    own_outputs = range(frames)
    carry_outputs = range(frames, frames + taps_count - 1)
    totals[...] = jnp.zeros_like(totals)
    rows_b[...] = jnp.zeros_like(rows_b)
    load(0).wait()
    turn(0, turned_a)

    @pl.when(half == 0)
    def _():
        pl.semaphore_wait(barrier, stations)
        for j in range(half_steps):
            give(j).start()

    def own_ready(i):
        @pl.when(jnp.logical_or(half == 1, i >= half_steps // 2))
        def _():
            arrived(i)

        @pl.when(jnp.logical_and(half == 0, i == 1))
        def _():
            near.start()

        @pl.when(jnp.logical_and(half == 1, i == half_steps - 1))
        def _():
            give(0).wait_recv()

    def carry_ready(i):
        @pl.when(half == 0)
        def _():
            arrived(i)

        @pl.when(half == 1)
        def _():
            give(2 * i + 1).wait_recv()

            @pl.when(2 * i + 2 < half_steps)
            def _():
                give(2 * i + 2).wait_recv()

    def phase(p, carry):
        carrying = jnp.where(half == p, half_steps // 2, 0)
        owning = jnp.where(p == 0, half_steps, 0)
        sweep(
            half_steps, carrying, half * fft_len, half * (fft_len // 2), carry_outputs,
            1, 1 - half, 0, carry_ready, False, half == 0,
        )
        sweep(steps, owning, 0, 0, own_outputs, 0, 1 - half, half * fft_len, own_ready, True, half == 1)
        return carry

    lax.fori_loop(0, 2, phase, 0)
    transform(rows_b, half_steps - 1, half)

    @pl.when(half == 1)
    def _():
        pl.semaphore_wait(barrier, stations)

    load_flags.wait()
    band = stations * per_group
    channel = lax.broadcasted_iota(jnp.int32, (band, columns), 0)
    column = lax.broadcasted_iota(jnp.int32, (band, columns), 1)
    spread = (channel == column // group_width * per_group + column % per_group).astype(jnp.bfloat16)
    flag_rows = flags[...].astype(jnp.float32).astype(jnp.bfloat16)
    both = jnp.dot(flag_rows, spread, preferred_element_type=jnp.float32)
    valid[...] = jnp.where(half == 0, both[:frames], both[frames:])

    lane = lax.broadcasted_iota(jnp.int32, (8, columns), 1)
    target = lane % group_width
    for g in range(stations):
        target = jnp.where(lane // group_width == g, target + owner_ref[g] * group_width, target)
    target = target[:1]
    mask = valid[...].astype(jnp.bfloat16)

    def weigh(values, low, high):
        count = high - low
        shaped = values.astype(jnp.bfloat16).reshape(count, inputs, columns)
        spectra[low * inputs : high * inputs, :] = (shaped * mask[low:high, None, :]).reshape(
            count * inputs, columns
        )

    @pl.when(half == 0)
    def _():
        weigh(totals[0] * sign, 0, frames)

    @pl.when(half == 1)
    def _():
        near.wait_recv()
        carried = carry_rows // inputs
        weigh((totals[0, :carry_rows, :] + totals[1, :carry_rows, :]) * sign + earlier[:carry_rows, :], 0, carried)
        weigh(totals[0, carry_rows:, :] * sign, carried, frames)

    slot = lax.broadcasted_iota(jnp.int32, (inputs, LANES), 1) // group_width

    def turn_copy(d):
        to = lax.rem(me + d, stations)
        return pltpu.make_async_remote_copy(
            src_ref=outgoing.at[to],
            dst_ref=received.at[me],
            send_sem=send_sem.at[d],
            recv_sem=recv_sem.at[d],
            device_id={"stn": to},
            device_id_type=MESH,
        )

    def arrange(order, carry):
        b = lax.rem(order + 1 + me // per_lane, stations // per_lane)
        row = lax.broadcasted_iota(jnp.int32, (LANES, columns), 0) + b * LANES
        picked = (row == target).astype(jnp.bfloat16)
        block = lax.dot_general(
            spectra[...], picked, (((1,), (1,)), ((), ())), preferred_element_type=jnp.float32
        )
        for r in range(per_lane):
            for quad in range(frames // per_lane):
                joined = jnp.zeros((inputs, LANES), jnp.float32)
                for t in range(per_lane):
                    first = (quad * per_lane + t) * inputs
                    piece = block[first : first + inputs, :]
                    if t != r:
                        piece = pltpu.roll(piece, ((t - r) * group_width) % LANES, 1)
                    joined = jnp.where(slot == t, piece, joined)
                outgoing[b * per_lane + r, :, quad * LANES : (quad + 1) * LANES] = joined.astype(
                    jnp.bfloat16
                )
        for r in range(per_lane):
            to = b * per_lane + r

            @pl.when(to != me)
            def _():
                turn_copy(lax.rem(to - me + stations, stations)).start()

        return carry

    lax.fori_loop(0, stations // per_lane, arrange, 0)

    received[me] = outgoing[me]

    def arrive(d, carry):
        turn_copy(d).wait_recv()
        return carry

    lax.fori_loop(1, stations, arrive, 0)

    total_inputs = stations * inputs
    length = frames * group_width
    per_block = ROW_BLOCK // inputs
    plane = lax.broadcasted_iota(jnp.int32, (ROW_BLOCK, length), 1) // per_group % 2
    everything = received[...].reshape(total_inputs, length)

    def correlate(b, carry):
        left = received[pl.ds(b * per_block, per_block)].reshape(ROW_BLOCK, length)
        full = left.astype(jnp.float32)
        turned = jnp.where(
            plane == 0, pltpu.roll(full, length - per_group, 1), -pltpu.roll(full, per_group, 1)
        ).astype(jnp.bfloat16)
        pair = jnp.concatenate([left, turned], axis=0)
        product = lax.dot_general(
            pair, everything, (((1,), (1,)), ((), ())), preferred_element_type=jnp.float32
        )
        products[b] = product.reshape(2, ROW_BLOCK, total_inputs)
        return carry

    blocks = out_ref.shape[0]
    last = pltpu.make_async_remote_copy(
        src_ref=products.at[pl.ds((1 - half) * blocks, blocks)],
        dst_ref=other,
        send_sem=final_sem.at[0],
        recv_sem=final_sem.at[1],
        device_id={"tim": 1 - half},
        device_id_type=MESH,
    )
    lax.fori_loop((1 - half) * blocks, (2 - half) * blocks, correlate, 0)
    last.start()
    lax.fori_loop(half * blocks, (1 + half) * blocks, correlate, 0)

    def sent(d, carry):
        turn_copy(d).wait_send()
        return carry

    lax.fori_loop(1, stations, sent, 0)

    @pl.when(half == 0)
    def _():
        near.wait_send()
        for j in range(half_steps):
            give(j).wait_send()

    last.wait()
    normaliser = 1.0 / (per_group * frames * 2)
    out_ref[...] = (products[pl.ds(half * blocks, blocks)] + other[...]) * normaliser


def arrange_planes(blocks_ref, out_ref):
    blocks, planes, rows, _ = blocks_ref.shape
    for b in range(blocks):
        for p in range(planes):
            out_ref[b * rows : (b + 1) * rows, p, :] = blocks_ref[b, p]


def per_device(samples, taps, flags, group_owner):
    inputs, frames, fft_len = samples.shape
    taps_count = taps.shape[0]
    stations = lax.axis_size("stn")
    band = flags.shape[0]
    per_group = band // stations
    columns = 2 * band
    total_inputs = stations * inputs
    blocks = total_inputs // ROW_BLOCK
    length = frames * 2 * per_group
    steps = fft_len // STEP_WIDTH
    chunks = STEP_WIDTH // LANES
    own_rows = frames * inputs
    scratch = [
        pltpu.VMEM((inputs, frames, fft_len + fft_len // 2), jnp.bfloat16),
        pltpu.VMEM((taps_count, fft_len), jnp.float32),
        pltpu.VMEM((fft_len // 2, columns), jnp.bfloat16),
        pltpu.VMEM((flags.shape[1], band), jnp.int32),
        pltpu.VMEM((own_rows // LANES, own_rows, LANES), jnp.bfloat16),
        pltpu.VMEM((chunks, own_rows, LANES), jnp.bfloat16),
        pltpu.VMEM((chunks, own_rows, LANES), jnp.bfloat16),
        pltpu.VMEM((chunks, own_rows, LANES), jnp.bfloat16),
        pltpu.VMEM((chunks, own_rows, LANES), jnp.bfloat16),
        pltpu.VMEM((2, own_rows, columns), jnp.float32),
        pltpu.VMEM((own_rows, columns), jnp.float32),
        pltpu.VMEM((frames, columns), jnp.float32),
        pltpu.VMEM((own_rows, columns), jnp.bfloat16),
        pltpu.VMEM((stations, inputs, length), jnp.bfloat16),
        pltpu.VMEM((stations, inputs, length), jnp.bfloat16),
        pltpu.VMEM((blocks, 2, ROW_BLOCK, total_inputs), jnp.float32),
        pltpu.VMEM((blocks // 2, 2, ROW_BLOCK, total_inputs), jnp.float32),
        pltpu.SemaphoreType.DMA((steps,)),
        pltpu.SemaphoreType.DMA((steps,)),
        pltpu.SemaphoreType.DMA((steps // 2,)),
        pltpu.SemaphoreType.DMA((1,)),
        pltpu.SemaphoreType.DMA((steps // 2,)),
        pltpu.SemaphoreType.DMA((steps // 2,)),
        pltpu.SemaphoreType.DMA((2,)),
        pltpu.SemaphoreType.DMA((stations,)),
        pltpu.SemaphoreType.DMA((stations,)),
        pltpu.SemaphoreType.DMA((2,)),
    ]
    shape = (blocks // 2, 2, ROW_BLOCK, total_inputs)
    kept = pltpu.VMEM if math.prod(shape) * 4 <= KEPT_LIMIT else jax.ShapeDtypeStruct
    table = jnp.asarray(table_constant(fft_len, stations, per_group))
    hbm = pl.BlockSpec(memory_space=pltpu.HBM)
    result = pl.pallas_call(
        functools.partial(kernel, (stations, per_group)),
        in_specs=[pl.BlockSpec(memory_space=pltpu.SMEM), hbm, hbm, hbm, hbm],
        out_specs=pl.BlockSpec(memory_space=pltpu.VMEM),
        out_shape=kept(shape, jnp.float32),
        scratch_shapes=scratch,
        compiler_params=pltpu.CompilerParams(
            collective_id=0, has_side_effects=True, vmem_limit_bytes=60 << 20
        ),
        name="correlator",
    )(group_owner, samples, taps, table, flags.T)
    ordered = pl.pallas_call(
        arrange_planes,
        in_specs=[pl.BlockSpec(memory_space=pltpu.VMEM)],
        out_specs=pl.BlockSpec(memory_space=pltpu.VMEM),
        out_shape=jax.ShapeDtypeStruct((total_inputs // 2, 2, total_inputs), jnp.float32),
        compiler_params=pltpu.CompilerParams(vmem_limit_bytes=result.size * 8 + (2 << 20)),
        name="planes",
    )(result)
    return ordered[None]


def solution(mesh):
    in_specs = (P(("grp", "stn"), "tim", None), P(), P("grp", None), P("grp"))
    out_specs = P(("grp", "stn"), "tim", None, None)
    return jax.shard_map(
        per_device, mesh=mesh, in_specs=in_specs, out_specs=out_specs, check_vma=False
    )
```

```python
import functools
import math

import jax
import jax.numpy as jnp
import numpy as np
from jax import lax
from jax.experimental import pallas as pl
from jax.experimental.pallas import tpu as pltpu
from jax.sharding import PartitionSpec as P

BAND_START = 1536
MESH = pl.DeviceIdType.MESH
LANES = 128
ROW_BLOCK = 64
STEP_WIDTH = 1024
DEPTH = 256
KEPT_LIMIT = 1 << 20


def half_table(fft_len, channels):
    bins = np.arange(channels, dtype=np.int64) + BAND_START
    index = (np.arange(fft_len // 2, dtype=np.int64)[:, None] * bins[None]) % fft_len
    angle = index * (2.0 * math.pi / fft_len)
    amplitude = 1.0 / math.sqrt(fft_len)
    return np.cos(angle) * amplitude, -np.sin(angle) * amplitude


def table_constant(fft_len, groups, per_group):
    planes = [p.reshape(-1, groups, 1, per_group) for p in half_table(fft_len, groups * per_group)]
    stacked = np.concatenate(planes, axis=2)
    return stacked.reshape(stacked.shape[0], -1).astype(np.float32).astype(jnp.bfloat16)


def tree_sum(weights, frame, pairs):
    if len(pairs) == 1:
        return weights[pairs[0][0]] * frame[pairs[0][1]]
    middle = 1 << ((len(pairs) - 1).bit_length() - 1)
    return tree_sum(weights, frame, pairs[:middle]) + tree_sum(weights, frame, pairs[middle:])


def kernel(
    dims, owner_ref, samples_ref, taps_ref, table_ref, flags_ref, out_ref,
    wide, taps, table, flags, perm, turned, rows_a, rows_b, totals, earlier,
    valid, spectra, outgoing, received, products, other,
    load_sem, taps_sem, table_sem, flags_sem, give_sem, take_sem, near_sem, send_sem, recv_sem, final_sem,
):
    stations, per_group = dims
    inputs, frames, fft_len = samples_ref.shape
    taps_count = taps_ref.shape[0]
    carry_rows = (taps_count - 1) * inputs
    own_rows = frames * inputs
    group_width = 2 * per_group
    columns = stations * group_width
    per_lane = LANES // group_width
    steps = fft_len // STEP_WIDTH
    half_steps = steps // 2
    chunks = STEP_WIDTH // LANES
    me = lax.axis_index("stn")
    half = lax.axis_index("tim")
    barrier = pltpu.get_barrier_semaphore()

    def stretch(j, base=0):
        return pl.ds(pl.multiple_of(base + j * STEP_WIDTH, STEP_WIDTH), STEP_WIDTH)

    def load(j):
        return pltpu.make_async_copy(
            samples_ref.at[:, :, stretch(j)], wide.at[:, :, stretch(j)], load_sem.at[j]
        )

    def load_taps(j):
        return pltpu.make_async_copy(taps_ref.at[:, stretch(j)], taps.at[:, stretch(j)], taps_sem.at[j])

    def load_table(j):
        return pltpu.make_async_copy(table_ref.at[stretch(j)], table.at[stretch(j)], table_sem.at[j])

    load_flags = pltpu.make_async_copy(flags_ref, flags, flags_sem.at[0])

    def give(j):
        return pltpu.make_async_remote_copy(
            src_ref=samples_ref.at[:, :, stretch(j, fft_len // 2)],
            dst_ref=wide.at[:, :, stretch(j, fft_len)],
            send_sem=give_sem.at[j],
            recv_sem=take_sem.at[j],
            device_id={"tim": 1 - half},
            device_id_type=MESH,
        )

    for j in range(steps):
        load(j).start()
        load_taps(j).start()
        if j < half_steps:
            load_table(j).start()
    load_flags.start()
    pl.semaphore_signal(barrier, inc=1, device_id={"tim": 1 - half}, device_id_type=MESH)

    def greet(d, carry):
        pl.semaphore_signal(
            barrier, inc=1, device_id={"stn": lax.rem(me + d, stations)}, device_id_type=MESH
        )
        return carry

    lax.fori_loop(1, stations, greet, 0)

    from_row = lax.broadcasted_iota(jnp.int32, (own_rows, own_rows), 0)
    from_column = lax.broadcasted_iota(jnp.int32, (own_rows, own_rows), 1)
    moving = (from_column == from_row % inputs * frames + from_row // inputs).astype(perm.dtype)
    for p in range(own_rows // LANES):
        perm[p] = moving[:, p * LANES : (p + 1) * LANES]

    pair_lanes = DEPTH // LANES
    pairs = chunks // pair_lanes

    def turn(offset, p):
        start = pl.multiple_of(offset + p * DEPTH, DEPTH)
        moving = jnp.concatenate([perm[q] for q in range(own_rows // LANES)], axis=1)
        block = wide[:, :, pl.ds(start, DEPTH)].reshape(own_rows, DEPTH)
        moved = jnp.dot(moving, block, preferred_element_type=jnp.float32).astype(jnp.bfloat16)
        for q in range(pair_lanes):
            turned[p * pair_lanes + q] = moved[:, q * LANES : (q + 1) * LANES]

    def filter_rows(j, base, into, outputs, p):
        for c in range(p * pair_lanes, (p + 1) * pair_lanes):
            lanes = pl.ds(pl.multiple_of(base + j * STEP_WIDTH + c * LANES, LANES), LANES)
            weights = [
                jnp.broadcast_to(taps[k : k + 1, lanes], (inputs, LANES)).astype(jnp.bfloat16)
                for k in range(taps_count)
            ]
            frame = [turned[c, s * inputs : (s + 1) * inputs, :] for s in range(frames)]
            for place, t in enumerate(outputs):
                first = t - (taps_count - 1)
                into[c, place * inputs : (place + 1) * inputs, :] = tree_sum(
                    weights, frame, [(k, first + k) for k in range(taps_count) if 0 <= first + k < frames]
                )

    def transform(rows, j, which, scale=None):
        stacked = jnp.concatenate([rows[c] for c in range(chunks)], axis=1)
        if columns <= DEPTH:
            totals[which] = add(totals[which], scale, stacked, table[stretch(j), :])
        else:

            def block(b, carry):
                to = pl.ds(pl.multiple_of(b * DEPTH, DEPTH), DEPTH)
                part = None if scale is None else scale[:, :DEPTH]
                totals[which, :, to] = add(totals[which, :, to], part, stacked, table[stretch(j), to])
                return carry

            lax.fori_loop(0, columns // DEPTH, block, 0)

    def add(held, scale, left, right):
        product = jnp.dot(left, right, preferred_element_type=jnp.float32)
        return held + product if scale is None else held * scale + product

    sign_row = lax.broadcasted_iota(jnp.int32, (1, columns), 1)
    bins = BAND_START + sign_row // group_width * per_group + sign_row % per_group
    sign = (1 - 2 * (bins % 2)).astype(jnp.float32)

    def sweep(count, trips, base, taps_base, outputs, total, other_total, follow, ready, flip, opening):
        def pair(i, carry):
            ready(i)
            even = 2 * i
            before = jnp.where(jnp.logical_and(opening, even == 0), 0, lax.rem(even + half_steps - 1, half_steps))
            scale = jnp.where(i == half_steps // 2, sign, 1.0) if flip else None
            for p in range(pairs):
                filter_rows(even, taps_base, rows_a, outputs, p)
                turn(base + (even + 1) * STEP_WIDTH, p)
            transform(rows_b, before, jnp.where(i == 0, other_total, total))
            after = jnp.where(even + 2 < count, base + (even + 2) * STEP_WIDTH, follow)
            for p in range(pairs):
                filter_rows(even + 1, taps_base, rows_b, outputs, p)
                turn(after, p)
            transform(rows_a, lax.rem(even, half_steps), total, scale)
            return carry

        lax.fori_loop(0, trips, pair, 0)

    def arrived(i):
        load(2 * i + 1).wait()

        @pl.when(2 * i + 2 < steps)
        def _():
            load(2 * i + 2).wait()

        for e in range(2):
            load_taps(2 * i + e).wait()

            @pl.when(i < half_steps // 2)
            def _():
                load_table(2 * i + e).wait()

    near = pltpu.make_async_remote_copy(
        src_ref=totals.at[1],
        dst_ref=earlier,
        send_sem=near_sem.at[0],
        recv_sem=near_sem.at[1],
        device_id={"tim": 1 - half},
        device_id_type=MESH,
    )
    own_outputs = range(frames)
    carry_outputs = range(frames, frames + taps_count - 1)
    totals[...] = jnp.zeros_like(totals)
    rows_b[...] = jnp.zeros_like(rows_b)
    load(0).wait()
    for p in range(pairs):
        turn(0, p)

    @pl.when(half == 0)
    def _():
        pl.semaphore_wait(barrier, stations)
        for j in range(half_steps):
            give(j).start()

    def own_ready(i):
        @pl.when(jnp.logical_or(half == 1, i >= half_steps // 2))
        def _():
            arrived(i)

        @pl.when(jnp.logical_and(half == 0, i == 1))
        def _():
            near.start()

        @pl.when(jnp.logical_and(half == 1, i == half_steps - 1))
        def _():
            give(0).wait_recv()

    def carry_ready(i):
        @pl.when(half == 0)
        def _():
            arrived(i)

        @pl.when(half == 1)
        def _():
            give(2 * i + 1).wait_recv()

            @pl.when(2 * i + 2 < half_steps)
            def _():
                give(2 * i + 2).wait_recv()

    def phase(p, carry):
        carrying = jnp.where(half == p, half_steps // 2, 0)
        owning = jnp.where(p == 0, half_steps, 0)
        sweep(
            half_steps, carrying, half * fft_len, half * (fft_len // 2), carry_outputs,
            1, 1 - half, 0, carry_ready, False, half == 0,
        )
        sweep(steps, owning, 0, 0, own_outputs, 0, 1 - half, half * fft_len, own_ready, True, half == 1)
        return carry

    lax.fori_loop(0, 2, phase, 0)
    transform(rows_b, half_steps - 1, half)

    @pl.when(half == 1)
    def _():
        pl.semaphore_wait(barrier, stations)

    load_flags.wait()
    band = stations * per_group
    channel = lax.broadcasted_iota(jnp.int32, (band, columns), 0)
    column = lax.broadcasted_iota(jnp.int32, (band, columns), 1)
    spread = (channel == column // group_width * per_group + column % per_group).astype(jnp.bfloat16)
    flag_rows = flags[...].astype(jnp.float32).astype(jnp.bfloat16)
    both = jnp.dot(flag_rows, spread, preferred_element_type=jnp.float32)
    valid[...] = jnp.where(half == 0, both[:frames], both[frames:])

    lane = lax.broadcasted_iota(jnp.int32, (8, columns), 1)
    target = lane % group_width
    for g in range(stations):
        target = jnp.where(lane // group_width == g, target + owner_ref[g] * group_width, target)
    target = target[:1]
    mask = valid[...].astype(jnp.bfloat16)

    def weigh(values, low, high):
        count = high - low
        shaped = values.astype(jnp.bfloat16).reshape(count, inputs, columns)
        spectra[low * inputs : high * inputs, :] = (shaped * mask[low:high, None, :]).reshape(
            count * inputs, columns
        )

    @pl.when(half == 0)
    def _():
        weigh(totals[0] * sign, 0, frames)

    @pl.when(half == 1)
    def _():
        near.wait_recv()
        carried = carry_rows // inputs
        weigh((totals[0, :carry_rows, :] + totals[1, :carry_rows, :]) * sign + earlier[:carry_rows, :], 0, carried)
        weigh(totals[0, carry_rows:, :] * sign, carried, frames)

    slot = lax.broadcasted_iota(jnp.int32, (inputs, LANES), 1) // group_width

    def turn_copy(d):
        to = lax.rem(me + d, stations)
        return pltpu.make_async_remote_copy(
            src_ref=outgoing.at[to],
            dst_ref=received.at[me],
            send_sem=send_sem.at[d],
            recv_sem=recv_sem.at[d],
            device_id={"stn": to},
            device_id_type=MESH,
        )

    def arrange(order, carry):
        b = lax.rem(order + 1 + me // per_lane, stations // per_lane)
        row = lax.broadcasted_iota(jnp.int32, (LANES, columns), 0) + b * LANES
        picked = (row == target).astype(jnp.bfloat16)
        block = lax.dot_general(
            spectra[...], picked, (((1,), (1,)), ((), ())), preferred_element_type=jnp.float32
        )
        for r in range(per_lane):
            for quad in range(frames // per_lane):
                joined = jnp.zeros((inputs, LANES), jnp.float32)
                for t in range(per_lane):
                    first = (quad * per_lane + t) * inputs
                    piece = block[first : first + inputs, :]
                    if t != r:
                        piece = pltpu.roll(piece, ((t - r) * group_width) % LANES, 1)
                    joined = jnp.where(slot == t, piece, joined)
                outgoing[b * per_lane + r, :, quad * LANES : (quad + 1) * LANES] = joined.astype(
                    jnp.bfloat16
                )
        for r in range(per_lane):
            to = b * per_lane + r

            @pl.when(to != me)
            def _():
                turn_copy(lax.rem(to - me + stations, stations)).start()

        return carry

    lax.fori_loop(0, stations // per_lane, arrange, 0)

    received[me] = outgoing[me]

    def arrive(d, carry):
        turn_copy(d).wait_recv()
        return carry

    lax.fori_loop(1, stations, arrive, 0)

    total_inputs = stations * inputs
    length = frames * group_width
    per_block = ROW_BLOCK // inputs
    plane = lax.broadcasted_iota(jnp.int32, (ROW_BLOCK, length), 1) // per_group % 2
    everything = received[...].reshape(total_inputs, length)

    def correlate(b, carry):
        left = received[pl.ds(b * per_block, per_block)].reshape(ROW_BLOCK, length)
        full = left.astype(jnp.float32)
        turned = jnp.where(
            plane == 0, pltpu.roll(full, length - per_group, 1), -pltpu.roll(full, per_group, 1)
        ).astype(jnp.bfloat16)
        pair = jnp.concatenate([left, turned], axis=0)
        product = lax.dot_general(
            pair, everything, (((1,), (1,)), ((), ())), preferred_element_type=jnp.float32
        )
        products[b] = product.reshape(2, ROW_BLOCK, total_inputs)
        return carry

    blocks = out_ref.shape[0]
    last = pltpu.make_async_remote_copy(
        src_ref=products.at[pl.ds((1 - half) * blocks, blocks)],
        dst_ref=other,
        send_sem=final_sem.at[0],
        recv_sem=final_sem.at[1],
        device_id={"tim": 1 - half},
        device_id_type=MESH,
    )
    lax.fori_loop((1 - half) * blocks, (2 - half) * blocks, correlate, 0)
    last.start()
    lax.fori_loop(half * blocks, (1 + half) * blocks, correlate, 0)

    def sent(d, carry):
        turn_copy(d).wait_send()
        return carry

    lax.fori_loop(1, stations, sent, 0)

    @pl.when(half == 0)
    def _():
        near.wait_send()
        for j in range(half_steps):
            give(j).wait_send()

    last.wait()
    normaliser = 1.0 / (per_group * frames * 2)
    out_ref[...] = (products[pl.ds(half * blocks, blocks)] + other[...]) * normaliser


def arrange_planes(blocks_ref, out_ref):
    blocks, planes, rows, _ = blocks_ref.shape
    for b in range(blocks):
        for p in range(planes):
            out_ref[b * rows : (b + 1) * rows, p, :] = blocks_ref[b, p]


def per_device(samples, taps, flags, group_owner):
    inputs, frames, fft_len = samples.shape
    taps_count = taps.shape[0]
    stations = lax.axis_size("stn")
    band = flags.shape[0]
    per_group = band // stations
    columns = 2 * band
    total_inputs = stations * inputs
    blocks = total_inputs // ROW_BLOCK
    length = frames * 2 * per_group
    steps = fft_len // STEP_WIDTH
    chunks = STEP_WIDTH // LANES
    own_rows = frames * inputs
    scratch = [
        pltpu.VMEM((inputs, frames, fft_len + fft_len // 2), jnp.bfloat16),
        pltpu.VMEM((taps_count, fft_len), jnp.float32),
        pltpu.VMEM((fft_len // 2, columns), jnp.bfloat16),
        pltpu.VMEM((flags.shape[1], band), jnp.int32),
        pltpu.VMEM((own_rows // LANES, own_rows, LANES), jnp.bfloat16),
        pltpu.VMEM((chunks, own_rows, LANES), jnp.bfloat16),
        pltpu.VMEM((chunks, own_rows, LANES), jnp.bfloat16),
        pltpu.VMEM((chunks, own_rows, LANES), jnp.bfloat16),
        pltpu.VMEM((2, own_rows, columns), jnp.float32),
        pltpu.VMEM((own_rows, columns), jnp.float32),
        pltpu.VMEM((frames, columns), jnp.float32),
        pltpu.VMEM((own_rows, columns), jnp.bfloat16),
        pltpu.VMEM((stations, inputs, length), jnp.bfloat16),
        pltpu.VMEM((stations, inputs, length), jnp.bfloat16),
        pltpu.VMEM((blocks, 2, ROW_BLOCK, total_inputs), jnp.float32),
        pltpu.VMEM((blocks // 2, 2, ROW_BLOCK, total_inputs), jnp.float32),
        pltpu.SemaphoreType.DMA((steps,)),
        pltpu.SemaphoreType.DMA((steps,)),
        pltpu.SemaphoreType.DMA((steps // 2,)),
        pltpu.SemaphoreType.DMA((1,)),
        pltpu.SemaphoreType.DMA((steps // 2,)),
        pltpu.SemaphoreType.DMA((steps // 2,)),
        pltpu.SemaphoreType.DMA((2,)),
        pltpu.SemaphoreType.DMA((stations,)),
        pltpu.SemaphoreType.DMA((stations,)),
        pltpu.SemaphoreType.DMA((2,)),
    ]
    shape = (blocks // 2, 2, ROW_BLOCK, total_inputs)
    kept = pltpu.VMEM if math.prod(shape) * 4 <= KEPT_LIMIT else jax.ShapeDtypeStruct
    table = jnp.asarray(table_constant(fft_len, stations, per_group))
    hbm = pl.BlockSpec(memory_space=pltpu.HBM)
    result = pl.pallas_call(
        functools.partial(kernel, (stations, per_group)),
        in_specs=[pl.BlockSpec(memory_space=pltpu.SMEM), hbm, hbm, hbm, hbm],
        out_specs=pl.BlockSpec(memory_space=pltpu.VMEM),
        out_shape=kept(shape, jnp.float32),
        scratch_shapes=scratch,
        compiler_params=pltpu.CompilerParams(
            collective_id=0, has_side_effects=True, vmem_limit_bytes=60 << 20
        ),
        name="correlator",
    )(group_owner, samples, taps, table, flags.T)
    ordered = pl.pallas_call(
        arrange_planes,
        in_specs=[pl.BlockSpec(memory_space=pltpu.VMEM)],
        out_specs=pl.BlockSpec(memory_space=pltpu.VMEM),
        out_shape=jax.ShapeDtypeStruct((total_inputs // 2, 2, total_inputs), jnp.float32),
        compiler_params=pltpu.CompilerParams(vmem_limit_bytes=result.size * 8 + (2 << 20)),
        name="planes",
    )(result)
    return ordered[None]


def solution(mesh):
    in_specs = (P(("grp", "stn"), "tim", None), P(), P("grp", None), P("grp"))
    out_specs = P(("grp", "stn"), "tim", None, None)
    return jax.shard_map(
        per_device, mesh=mesh, in_specs=in_specs, out_specs=out_specs, check_vma=False
    )
```

```python
import functools
import math

import jax
import jax.numpy as jnp
import numpy as np
from jax import lax
from jax.experimental import pallas as pl
from jax.experimental.pallas import tpu as pltpu
from jax.sharding import PartitionSpec as P

BAND_START = 1536
MESH = pl.DeviceIdType.MESH
LANES = 128
ROW_BLOCK = 64
STEP_WIDTH = 512
DEPTH = 256
GROUP = 4
KEPT_LIMIT = 1 << 20


def half_table(fft_len, channels):
    bins = np.arange(channels, dtype=np.int64) + BAND_START
    index = (np.arange(fft_len // 2, dtype=np.int64)[:, None] * bins[None]) % fft_len
    angle = index * (2.0 * math.pi / fft_len)
    amplitude = 1.0 / math.sqrt(fft_len)
    return np.cos(angle) * amplitude, -np.sin(angle) * amplitude


def table_constant(fft_len, groups, per_group):
    planes = [p.reshape(-1, groups, 1, per_group) for p in half_table(fft_len, groups * per_group)]
    stacked = np.concatenate(planes, axis=2)
    return stacked.reshape(stacked.shape[0], -1).astype(np.float32).astype(jnp.bfloat16)


def tree_sum(weights, frame, pairs):
    if len(pairs) == 1:
        return weights[pairs[0][0]] * frame[pairs[0][1]]
    middle = 1 << ((len(pairs) - 1).bit_length() - 1)
    return tree_sum(weights, frame, pairs[:middle]) + tree_sum(weights, frame, pairs[middle:])


def kernel(
    dims, owner_ref, samples_ref, taps_ref, table_ref, flags_ref, out_ref,
    wide, taps, table, flags, perm, turned, rows_b, totals, earlier,
    valid, spectra, outgoing, received, products, other,
    load_sem, taps_sem, table_sem, flags_sem, give_sem, take_sem, near_sem, send_sem, recv_sem, final_sem,
):
    stations, per_group = dims
    inputs, frames, fft_len = samples_ref.shape
    taps_count = taps_ref.shape[0]
    carry_rows = (taps_count - 1) * inputs
    own_rows = frames * inputs
    group_width = 2 * per_group
    columns = stations * group_width
    per_lane = LANES // group_width
    steps = fft_len // STEP_WIDTH
    half_steps = steps // 2
    chunks = STEP_WIDTH // LANES
    me = lax.axis_index("stn")
    half = lax.axis_index("tim")
    barrier = pltpu.get_barrier_semaphore()

    def stretch(j, base=0):
        return pl.ds(pl.multiple_of(base + j * STEP_WIDTH, STEP_WIDTH), STEP_WIDTH)

    def load(j):
        return pltpu.make_async_copy(
            samples_ref.at[:, :, stretch(j)], wide.at[:, :, stretch(j)], load_sem.at[j]
        )

    def load_taps(j):
        return pltpu.make_async_copy(taps_ref.at[:, stretch(j)], taps.at[:, stretch(j)], taps_sem.at[j])

    def load_table(j):
        return pltpu.make_async_copy(table_ref.at[stretch(j)], table.at[stretch(j)], table_sem.at[j])

    load_flags = pltpu.make_async_copy(flags_ref, flags, flags_sem.at[0])

    def give(j):
        return pltpu.make_async_remote_copy(
            src_ref=samples_ref.at[:, :, stretch(j, fft_len // 2)],
            dst_ref=wide.at[:, :, stretch(j, fft_len)],
            send_sem=give_sem.at[j],
            recv_sem=take_sem.at[j],
            device_id={"tim": 1 - half},
            device_id_type=MESH,
        )

    for j in range(steps):
        load(j).start()
        load_taps(j).start()
        if j < half_steps:
            load_table(j).start()
    load_flags.start()
    pl.semaphore_signal(barrier, inc=1, device_id={"tim": 1 - half}, device_id_type=MESH)

    def greet(d, carry):
        pl.semaphore_signal(
            barrier, inc=1, device_id={"stn": lax.rem(me + d, stations)}, device_id_type=MESH
        )
        return carry

    lax.fori_loop(1, stations, greet, 0)

    from_row = lax.broadcasted_iota(jnp.int32, (own_rows, own_rows), 0)
    from_column = lax.broadcasted_iota(jnp.int32, (own_rows, own_rows), 1)
    moving = (from_column == from_row % inputs * frames + from_row // inputs).astype(perm.dtype)
    for p in range(own_rows // LANES):
        perm[p] = moving[:, p * LANES : (p + 1) * LANES]

    pair_lanes = DEPTH // LANES
    pairs = chunks // pair_lanes

    def turn(offset, p):
        start = pl.multiple_of(offset + p * DEPTH, DEPTH)
        moving = jnp.concatenate([perm[q] for q in range(own_rows // LANES)], axis=1)
        block = wide[:, :, pl.ds(start, DEPTH)].reshape(own_rows, DEPTH)
        moved = jnp.dot(moving, block, preferred_element_type=jnp.float32).astype(jnp.bfloat16)
        for q in range(pair_lanes):
            turned[p * pair_lanes + q] = moved[:, q * LANES : (q + 1) * LANES]

    def filter_rows(j, base, into, outputs, p):
        blocks = []
        for c in range(p * pair_lanes, (p + 1) * pair_lanes):
            lanes = pl.ds(pl.multiple_of(base + j * STEP_WIDTH + c * LANES, LANES), LANES)
            weights = [
                jnp.broadcast_to(taps[k : k + 1, lanes], (inputs, LANES)).astype(jnp.bfloat16)
                for k in range(taps_count)
            ]
            frame = [turned[c, s * inputs : (s + 1) * inputs, :] for s in range(frames)]
            made = []
            for t in outputs:
                first = t - (taps_count - 1)
                pairs_of = [(k, first + k) for k in range(taps_count) if 0 <= first + k < frames]
                made.append(tree_sum(weights, frame, pairs_of))
            if into is not None:
                for place, value in enumerate(made):
                    into[c, place * inputs : (place + 1) * inputs, :] = value
            blocks.append(jnp.concatenate(made, axis=0))
        return blocks

    def transform(blocks, j, which, scale=None):
        stacked = jnp.concatenate(blocks, axis=1)
        high = stacked.shape[0]
        if columns <= DEPTH:
            totals[which, :high] = add(totals[which, :high], scale, stacked, table[stretch(j), :])
        else:

            def block(b, carry):
                to = pl.ds(pl.multiple_of(b * DEPTH, DEPTH), DEPTH)
                part = None if scale is None else scale[:, :DEPTH]
                totals[which, :high, to] = add(totals[which, :high, to], part, stacked, table[stretch(j), to])
                return carry

            lax.fori_loop(0, columns // DEPTH, block, 0)

    def held():
        return [rows_b[c] for c in range(chunks)]

    def add(before, scale, left, right):
        product = jnp.dot(left, right, preferred_element_type=jnp.float32)
        return before + product if scale is None else before * scale + product

    sign_row = lax.broadcasted_iota(jnp.int32, (1, columns), 1)
    bins = BAND_START + sign_row // group_width * per_group + sign_row % per_group
    sign = (1 - 2 * (bins % 2)).astype(jnp.float32)

    def sweep(count, trips, base, taps_base, outputs, total, other_total, follow, ready, flip, opening):
        def group(i, carry):
            ready(i)
            for e in range(GROUP):
                now = GROUP * i + e
                after = base + (now + 1) * STEP_WIDTH
                if e + 1 == GROUP:
                    after = jnp.where(now + 1 < count, after, follow)
                blocks = []
                for p in range(pairs):
                    blocks += filter_rows(now, taps_base, rows_b if e + 1 == GROUP else None, outputs, p)
                    turn(after, p)
                if e == 0:
                    before = jnp.where(
                        jnp.logical_and(opening, i == 0), 0, lax.rem(now + half_steps - 1, half_steps)
                    )
                    transform(held(), before, jnp.where(i == 0, other_total, total))
                if e + 1 < GROUP:
                    scale = jnp.where(now == half_steps, sign, 1.0) if flip and half_steps % GROUP == e else None
                    transform(blocks, lax.rem(now, half_steps), total, scale)
            return carry

        lax.fori_loop(0, trips, group, 0)

    def arrived(i):
        for e in range(GROUP):
            load_taps(GROUP * i + e).wait()

            @pl.when(GROUP * i + e + 1 < steps)
            def _():
                load(GROUP * i + e + 1).wait()

            @pl.when(i < half_steps // GROUP)
            def _():
                load_table(GROUP * i + e).wait()

    near = pltpu.make_async_remote_copy(
        src_ref=totals.at[1],
        dst_ref=earlier,
        send_sem=near_sem.at[0],
        recv_sem=near_sem.at[1],
        device_id={"tim": 1 - half},
        device_id_type=MESH,
    )
    own_outputs = range(frames)
    carry_outputs = range(frames, frames + taps_count - 1)
    totals[...] = jnp.zeros_like(totals)
    rows_b[...] = jnp.zeros_like(rows_b)
    load(0).wait()
    for p in range(pairs):
        turn(0, p)

    @pl.when(half == 0)
    def _():
        pl.semaphore_wait(barrier, stations)
        for j in range(half_steps):
            give(j).start()

    def own_ready(i):
        @pl.when(jnp.logical_or(half == 1, i >= half_steps // GROUP))
        def _():
            arrived(i)

        @pl.when(jnp.logical_and(half == 0, i == 1))
        def _():
            near.start()

        @pl.when(jnp.logical_and(half == 1, i == steps // GROUP - 1))
        def _():
            give(0).wait_recv()

    def carry_ready(i):
        @pl.when(half == 0)
        def _():
            arrived(i)

        @pl.when(half == 1)
        def _():
            for e in range(GROUP):

                @pl.when(GROUP * i + e + 1 < half_steps)
                def _():
                    give(GROUP * i + e + 1).wait_recv()

    def phase(p, carry):
        carrying = jnp.where(half == p, half_steps // GROUP, 0)
        owning = jnp.where(p == 0, steps // GROUP, 0)
        sweep(
            half_steps, carrying, half * fft_len, half * (fft_len // 2), carry_outputs,
            1, 1 - half, 0, carry_ready, False, half == 0,
        )
        sweep(steps, owning, 0, 0, own_outputs, 0, 1 - half, half * fft_len, own_ready, True, half == 1)
        return carry

    lax.fori_loop(0, 2, phase, 0)
    transform(held(), half_steps - 1, half)

    @pl.when(half == 1)
    def _():
        pl.semaphore_wait(barrier, stations)

    load_flags.wait()
    band = stations * per_group
    channel = lax.broadcasted_iota(jnp.int32, (band, columns), 0)
    column = lax.broadcasted_iota(jnp.int32, (band, columns), 1)
    spread = (channel == column // group_width * per_group + column % per_group).astype(jnp.bfloat16)
    flag_rows = flags[...].astype(jnp.float32).astype(jnp.bfloat16)
    both = jnp.dot(flag_rows, spread, preferred_element_type=jnp.float32)
    valid[...] = jnp.where(half == 0, both[:frames], both[frames:])

    lane = lax.broadcasted_iota(jnp.int32, (8, columns), 1)
    target = lane % group_width
    for g in range(stations):
        target = jnp.where(lane // group_width == g, target + owner_ref[g] * group_width, target)
    target = target[:1]
    mask = valid[...].astype(jnp.bfloat16)

    def weigh(values, low, high):
        count = high - low
        shaped = values.astype(jnp.bfloat16).reshape(count, inputs, columns)
        spectra[low * inputs : high * inputs, :] = (shaped * mask[low:high, None, :]).reshape(
            count * inputs, columns
        )

    @pl.when(half == 0)
    def _():
        weigh(totals[0] * sign, 0, frames)

    @pl.when(half == 1)
    def _():
        near.wait_recv()
        carried = carry_rows // inputs
        weigh((totals[0, :carry_rows, :] + totals[1, :carry_rows, :]) * sign + earlier[:carry_rows, :], 0, carried)
        weigh(totals[0, carry_rows:, :] * sign, carried, frames)

    slot = lax.broadcasted_iota(jnp.int32, (inputs, LANES), 1) // group_width

    def turn_copy(d):
        to = lax.rem(me + d, stations)
        return pltpu.make_async_remote_copy(
            src_ref=outgoing.at[to],
            dst_ref=received.at[me],
            send_sem=send_sem.at[d],
            recv_sem=recv_sem.at[d],
            device_id={"stn": to},
            device_id_type=MESH,
        )

    def arrange(order, carry):
        b = lax.rem(order + 1 + me // per_lane, stations // per_lane)
        row = lax.broadcasted_iota(jnp.int32, (LANES, columns), 0) + b * LANES
        picked = (row == target).astype(jnp.bfloat16)
        block = lax.dot_general(
            spectra[...], picked, (((1,), (1,)), ((), ())), preferred_element_type=jnp.float32
        )
        for r in range(per_lane):
            for quad in range(frames // per_lane):
                joined = jnp.zeros((inputs, LANES), jnp.float32)
                for t in range(per_lane):
                    first = (quad * per_lane + t) * inputs
                    piece = block[first : first + inputs, :]
                    if t != r:
                        piece = pltpu.roll(piece, ((t - r) * group_width) % LANES, 1)
                    joined = jnp.where(slot == t, piece, joined)
                outgoing[b * per_lane + r, :, quad * LANES : (quad + 1) * LANES] = joined.astype(
                    jnp.bfloat16
                )
        for r in range(per_lane):
            to = b * per_lane + r

            @pl.when(to != me)
            def _():
                turn_copy(lax.rem(to - me + stations, stations)).start()

        return carry

    lax.fori_loop(0, stations // per_lane, arrange, 0)

    received[me] = outgoing[me]

    def arrive(d, carry):
        turn_copy(d).wait_recv()
        return carry

    lax.fori_loop(1, stations, arrive, 0)

    total_inputs = stations * inputs
    length = frames * group_width
    per_block = ROW_BLOCK // inputs
    plane = lax.broadcasted_iota(jnp.int32, (ROW_BLOCK, length), 1) // per_group % 2
    everything = received[...].reshape(total_inputs, length)

    def correlate(b, carry):
        left = received[pl.ds(b * per_block, per_block)].reshape(ROW_BLOCK, length)
        full = left.astype(jnp.float32)
        turned = jnp.where(
            plane == 0, pltpu.roll(full, length - per_group, 1), -pltpu.roll(full, per_group, 1)
        ).astype(jnp.bfloat16)
        pair = jnp.concatenate([left, turned], axis=0)
        product = lax.dot_general(
            pair, everything, (((1,), (1,)), ((), ())), preferred_element_type=jnp.float32
        )
        products[b] = product.reshape(2, ROW_BLOCK, total_inputs)
        return carry

    blocks = out_ref.shape[0]
    last = pltpu.make_async_remote_copy(
        src_ref=products.at[pl.ds((1 - half) * blocks, blocks)],
        dst_ref=other,
        send_sem=final_sem.at[0],
        recv_sem=final_sem.at[1],
        device_id={"tim": 1 - half},
        device_id_type=MESH,
    )
    lax.fori_loop((1 - half) * blocks, (2 - half) * blocks, correlate, 0)
    last.start()
    lax.fori_loop(half * blocks, (1 + half) * blocks, correlate, 0)

    def sent(d, carry):
        turn_copy(d).wait_send()
        return carry

    lax.fori_loop(1, stations, sent, 0)

    @pl.when(half == 0)
    def _():
        near.wait_send()
        for j in range(half_steps):
            give(j).wait_send()

    last.wait()
    normaliser = 1.0 / (per_group * frames * 2)
    out_ref[...] = (products[pl.ds(half * blocks, blocks)] + other[...]) * normaliser


def arrange_planes(blocks_ref, out_ref):
    blocks, planes, rows, _ = blocks_ref.shape
    for b in range(blocks):
        for p in range(planes):
            out_ref[b * rows : (b + 1) * rows, p, :] = blocks_ref[b, p]


def per_device(samples, taps, flags, group_owner):
    inputs, frames, fft_len = samples.shape
    taps_count = taps.shape[0]
    stations = lax.axis_size("stn")
    band = flags.shape[0]
    per_group = band // stations
    columns = 2 * band
    total_inputs = stations * inputs
    blocks = total_inputs // ROW_BLOCK
    length = frames * 2 * per_group
    steps = fft_len // STEP_WIDTH
    chunks = STEP_WIDTH // LANES
    own_rows = frames * inputs
    scratch = [
        pltpu.VMEM((inputs, frames, fft_len + fft_len // 2), jnp.bfloat16),
        pltpu.VMEM((taps_count, fft_len), jnp.float32),
        pltpu.VMEM((fft_len // 2, columns), jnp.bfloat16),
        pltpu.VMEM((flags.shape[1], band), jnp.int32),
        pltpu.VMEM((own_rows // LANES, own_rows, LANES), jnp.bfloat16),
        pltpu.VMEM((chunks, own_rows, LANES), jnp.bfloat16),
        pltpu.VMEM((chunks, own_rows, LANES), jnp.bfloat16),
        pltpu.VMEM((2, own_rows, columns), jnp.float32),
        pltpu.VMEM((own_rows, columns), jnp.float32),
        pltpu.VMEM((frames, columns), jnp.float32),
        pltpu.VMEM((own_rows, columns), jnp.bfloat16),
        pltpu.VMEM((stations, inputs, length), jnp.bfloat16),
        pltpu.VMEM((stations, inputs, length), jnp.bfloat16),
        pltpu.VMEM((blocks, 2, ROW_BLOCK, total_inputs), jnp.float32),
        pltpu.VMEM((blocks // 2, 2, ROW_BLOCK, total_inputs), jnp.float32),
        pltpu.SemaphoreType.DMA((steps,)),
        pltpu.SemaphoreType.DMA((steps,)),
        pltpu.SemaphoreType.DMA((steps // 2,)),
        pltpu.SemaphoreType.DMA((1,)),
        pltpu.SemaphoreType.DMA((steps // 2,)),
        pltpu.SemaphoreType.DMA((steps // 2,)),
        pltpu.SemaphoreType.DMA((2,)),
        pltpu.SemaphoreType.DMA((stations,)),
        pltpu.SemaphoreType.DMA((stations,)),
        pltpu.SemaphoreType.DMA((2,)),
    ]
    shape = (blocks // 2, 2, ROW_BLOCK, total_inputs)
    kept = pltpu.VMEM if math.prod(shape) * 4 <= KEPT_LIMIT else jax.ShapeDtypeStruct
    table = jnp.asarray(table_constant(fft_len, stations, per_group))
    hbm = pl.BlockSpec(memory_space=pltpu.HBM)
    result = pl.pallas_call(
        functools.partial(kernel, (stations, per_group)),
        in_specs=[pl.BlockSpec(memory_space=pltpu.SMEM), hbm, hbm, hbm, hbm],
        out_specs=pl.BlockSpec(memory_space=pltpu.VMEM),
        out_shape=kept(shape, jnp.float32),
        scratch_shapes=scratch,
        compiler_params=pltpu.CompilerParams(
            collective_id=0, has_side_effects=True, vmem_limit_bytes=60 << 20
        ),
        name="correlator",
    )(group_owner, samples, taps, table, flags.T)
    ordered = pl.pallas_call(
        arrange_planes,
        in_specs=[pl.BlockSpec(memory_space=pltpu.VMEM)],
        out_specs=pl.BlockSpec(memory_space=pltpu.VMEM),
        out_shape=jax.ShapeDtypeStruct((total_inputs // 2, 2, total_inputs), jnp.float32),
        compiler_params=pltpu.CompilerParams(vmem_limit_bytes=result.size * 8 + (2 << 20)),
        name="planes",
    )(result)
    return ordered[None]


def solution(mesh):
    in_specs = (P(("grp", "stn"), "tim", None), P(), P("grp", None), P("grp"))
    out_specs = P(("grp", "stn"), "tim", None, None)
    return jax.shard_map(
        per_device, mesh=mesh, in_specs=in_specs, out_specs=out_specs, check_vma=False
    )
```

```python
import functools
import math

import jax
import jax.numpy as jnp
import numpy as np
from jax import lax
from jax.experimental import pallas as pl
from jax.experimental.pallas import tpu as pltpu
from jax.sharding import PartitionSpec as P

BAND_START = 1536
MESH = pl.DeviceIdType.MESH
LANES = 128
ROW_BLOCK = 64
STEP_WIDTH = 512
DEPTH = 256
GROUP = 4
KEPT_LIMIT = 1 << 20


def half_table(fft_len, channels):
    bins = np.arange(channels, dtype=np.int64) + BAND_START
    index = (np.arange(fft_len // 2, dtype=np.int64)[:, None] * bins[None]) % fft_len
    angle = index * (2.0 * math.pi / fft_len)
    amplitude = 1.0 / math.sqrt(fft_len)
    return np.cos(angle) * amplitude, -np.sin(angle) * amplitude


def table_constant(fft_len, groups, per_group):
    planes = [p.reshape(-1, groups, 1, per_group) for p in half_table(fft_len, groups * per_group)]
    stacked = np.concatenate(planes, axis=2)
    return stacked.reshape(stacked.shape[0], -1).astype(np.float32).astype(jnp.bfloat16)


def tree_sum(weights, frame, pairs):
    if len(pairs) == 1:
        return weights[pairs[0][0]] * frame[pairs[0][1]]
    middle = 1 << ((len(pairs) - 1).bit_length() - 1)
    return tree_sum(weights, frame, pairs[:middle]) + tree_sum(weights, frame, pairs[middle:])


def kernel(
    dims, owner_ref, samples_ref, taps_ref, table_ref, flags_ref, out_ref,
    wide, taps, table, flags, perm, turned, rows_b, totals, earlier,
    valid, spectra, outgoing, received, products, other,
    load_sem, taps_sem, table_sem, flags_sem, give_sem, take_sem, near_sem, send_sem, recv_sem, final_sem,
):
    stations, per_group = dims
    inputs, frames, fft_len = samples_ref.shape
    taps_count = taps_ref.shape[0]
    carry_rows = (taps_count - 1) * inputs
    own_rows = frames * inputs
    group_width = 2 * per_group
    columns = stations * group_width
    per_lane = LANES // group_width
    steps = fft_len // STEP_WIDTH
    half_steps = steps // 2
    chunks = STEP_WIDTH // LANES
    me = lax.axis_index("stn")
    half = lax.axis_index("tim")
    barrier = pltpu.get_barrier_semaphore()

    def stretch(j, base=0):
        return pl.ds(pl.multiple_of(base + j * STEP_WIDTH, STEP_WIDTH), STEP_WIDTH)

    def load(j):
        return pltpu.make_async_copy(
            samples_ref.at[:, :, stretch(j)], wide.at[j], load_sem.at[j]
        )

    def load_taps(j):
        return pltpu.make_async_copy(taps_ref.at[:, stretch(j)], taps.at[:, stretch(j)], taps_sem.at[j])

    def load_table(j):
        return pltpu.make_async_copy(table_ref.at[stretch(j)], table.at[stretch(j)], table_sem.at[j])

    load_flags = pltpu.make_async_copy(flags_ref, flags, flags_sem.at[0])

    def give(j):
        return pltpu.make_async_remote_copy(
            src_ref=samples_ref.at[:, :, stretch(j, fft_len // 2)],
            dst_ref=wide.at[steps + j],
            send_sem=give_sem.at[j],
            recv_sem=take_sem.at[j],
            device_id={"tim": 1 - half},
            device_id_type=MESH,
        )

    for j in range(steps):
        load(j).start()
        load_taps(j).start()
        if j < half_steps:
            load_table(j).start()
    load_flags.start()
    pl.semaphore_signal(barrier, inc=1, device_id={"tim": 1 - half}, device_id_type=MESH)

    def greet(d, carry):
        pl.semaphore_signal(
            barrier, inc=1, device_id={"stn": lax.rem(me + d, stations)}, device_id_type=MESH
        )
        return carry

    lax.fori_loop(1, stations, greet, 0)

    from_row = lax.broadcasted_iota(jnp.int32, (own_rows, own_rows), 0)
    from_column = lax.broadcasted_iota(jnp.int32, (own_rows, own_rows), 1)
    moving = (from_column == from_row % inputs * frames + from_row // inputs).astype(perm.dtype)
    for p in range(own_rows // LANES):
        perm[p] = moving[:, p * LANES : (p + 1) * LANES]

    pair_lanes = DEPTH // LANES
    pairs = chunks // pair_lanes

    def turn(offset, p):
        moving = jnp.concatenate([perm[q] for q in range(own_rows // LANES)], axis=1)
        block = wide[lax.div(offset, STEP_WIDTH), :, :, p * DEPTH : (p + 1) * DEPTH].reshape(own_rows, DEPTH)
        moved = jnp.dot(moving, block, preferred_element_type=jnp.float32).astype(jnp.bfloat16)
        for q in range(pair_lanes):
            turned[p * pair_lanes + q] = moved[:, q * LANES : (q + 1) * LANES]

    def filter_rows(j, base, into, outputs, p):
        blocks = []
        for c in range(p * pair_lanes, (p + 1) * pair_lanes):
            lanes = pl.ds(pl.multiple_of(base + j * STEP_WIDTH + c * LANES, LANES), LANES)
            weights = [
                jnp.broadcast_to(taps[k : k + 1, lanes], (inputs, LANES)).astype(jnp.bfloat16)
                for k in range(taps_count)
            ]
            frame = [turned[c, s * inputs : (s + 1) * inputs, :] for s in range(frames)]
            made = []
            for t in outputs:
                first = t - (taps_count - 1)
                pairs_of = [(k, first + k) for k in range(taps_count) if 0 <= first + k < frames]
                made.append(tree_sum(weights, frame, pairs_of))
            if into is not None:
                for place, value in enumerate(made):
                    into[c, place * inputs : (place + 1) * inputs, :] = value
            blocks.append(jnp.concatenate(made, axis=0))
        return blocks

    def transform(blocks, j, which, scale=None):
        stacked = jnp.concatenate(blocks, axis=1)
        high = stacked.shape[0]
        if columns <= DEPTH:
            totals[which, :high] = add(totals[which, :high], scale, stacked, table[stretch(j), :])
        else:

            def block(b, carry):
                to = pl.ds(pl.multiple_of(b * DEPTH, DEPTH), DEPTH)
                part = None if scale is None else scale[:, :DEPTH]
                totals[which, :high, to] = add(totals[which, :high, to], part, stacked, table[stretch(j), to])
                return carry

            lax.fori_loop(0, columns // DEPTH, block, 0)

    def held():
        return [rows_b[c] for c in range(chunks)]

    def add(before, scale, left, right):
        product = jnp.dot(left, right, preferred_element_type=jnp.float32)
        return before + product if scale is None else before * scale + product

    sign_row = lax.broadcasted_iota(jnp.int32, (1, columns), 1)
    bins = BAND_START + sign_row // group_width * per_group + sign_row % per_group
    sign = (1 - 2 * (bins % 2)).astype(jnp.float32)

    def sweep(count, trips, base, taps_base, outputs, total, other_total, follow, ready, flip, opening):
        def group(i, carry):
            ready(i)
            for e in range(GROUP):
                now = GROUP * i + e
                after = base + (now + 1) * STEP_WIDTH
                if e + 1 == GROUP:
                    after = jnp.where(now + 1 < count, after, follow)
                blocks = []
                for p in range(pairs):
                    blocks += filter_rows(now, taps_base, rows_b if e + 1 == GROUP else None, outputs, p)
                    turn(after, p)
                if e == 0:
                    before = jnp.where(
                        jnp.logical_and(opening, i == 0), 0, lax.rem(now + half_steps - 1, half_steps)
                    )
                    transform(held(), before, jnp.where(i == 0, other_total, total))
                if e + 1 < GROUP:
                    scale = jnp.where(now == half_steps, sign, 1.0) if flip and half_steps % GROUP == e else None
                    transform(blocks, lax.rem(now, half_steps), total, scale)
            return carry

        lax.fori_loop(0, trips, group, 0)

    def arrived(i):
        for e in range(GROUP):
            load_taps(GROUP * i + e).wait()

            @pl.when(GROUP * i + e + 1 < steps)
            def _():
                load(GROUP * i + e + 1).wait()

            @pl.when(i < half_steps // GROUP)
            def _():
                load_table(GROUP * i + e).wait()

    near = pltpu.make_async_remote_copy(
        src_ref=totals.at[1],
        dst_ref=earlier,
        send_sem=near_sem.at[0],
        recv_sem=near_sem.at[1],
        device_id={"tim": 1 - half},
        device_id_type=MESH,
    )
    own_outputs = range(frames)
    carry_outputs = range(frames, frames + taps_count - 1)
    totals[...] = jnp.zeros_like(totals)
    rows_b[...] = jnp.zeros_like(rows_b)
    load(0).wait()
    for p in range(pairs):
        turn(0, p)

    @pl.when(half == 0)
    def _():
        pl.semaphore_wait(barrier, stations)
        for j in range(half_steps):
            give(j).start()

    def own_ready(i):
        @pl.when(jnp.logical_or(half == 1, i >= half_steps // GROUP))
        def _():
            arrived(i)

        @pl.when(jnp.logical_and(half == 0, i == 1))
        def _():
            near.start()

        @pl.when(jnp.logical_and(half == 1, i == steps // GROUP - 1))
        def _():
            give(0).wait_recv()

    def carry_ready(i):
        @pl.when(half == 0)
        def _():
            arrived(i)

        @pl.when(half == 1)
        def _():
            for e in range(GROUP):

                @pl.when(GROUP * i + e + 1 < half_steps)
                def _():
                    give(GROUP * i + e + 1).wait_recv()

    def phase(p, carry):
        carrying = jnp.where(half == p, half_steps // GROUP, 0)
        owning = jnp.where(p == 0, steps // GROUP, 0)
        sweep(
            half_steps, carrying, half * fft_len, half * (fft_len // 2), carry_outputs,
            1, 1 - half, 0, carry_ready, False, half == 0,
        )
        sweep(steps, owning, 0, 0, own_outputs, 0, 1 - half, half * fft_len, own_ready, True, half == 1)
        return carry

    lax.fori_loop(0, 2, phase, 0)
    transform(held(), half_steps - 1, half)

    @pl.when(half == 1)
    def _():
        pl.semaphore_wait(barrier, stations)

    load_flags.wait()
    band = stations * per_group
    channel = lax.broadcasted_iota(jnp.int32, (band, columns), 0)
    column = lax.broadcasted_iota(jnp.int32, (band, columns), 1)
    spread = (channel == column // group_width * per_group + column % per_group).astype(jnp.bfloat16)
    flag_rows = flags[...].astype(jnp.float32).astype(jnp.bfloat16)
    both = jnp.dot(flag_rows, spread, preferred_element_type=jnp.float32)
    valid[...] = jnp.where(half == 0, both[:frames], both[frames:])

    lane = lax.broadcasted_iota(jnp.int32, (8, columns), 1)
    target = lane % group_width
    for g in range(stations):
        target = jnp.where(lane // group_width == g, target + owner_ref[g] * group_width, target)
    target = target[:1]
    mask = valid[...].astype(jnp.bfloat16)

    def weigh(values, low, high):
        count = high - low
        shaped = values.astype(jnp.bfloat16).reshape(count, inputs, columns)
        spectra[low * inputs : high * inputs, :] = (shaped * mask[low:high, None, :]).reshape(
            count * inputs, columns
        )

    @pl.when(half == 0)
    def _():
        weigh(totals[0] * sign, 0, frames)

    @pl.when(half == 1)
    def _():
        near.wait_recv()
        carried = carry_rows // inputs
        weigh((totals[0, :carry_rows, :] + totals[1, :carry_rows, :]) * sign + earlier[:carry_rows, :], 0, carried)
        weigh(totals[0, carry_rows:, :] * sign, carried, frames)

    slot = lax.broadcasted_iota(jnp.int32, (inputs, LANES), 1) // group_width

    def turn_copy(d):
        to = lax.rem(me + d, stations)
        return pltpu.make_async_remote_copy(
            src_ref=outgoing.at[to],
            dst_ref=received.at[me],
            send_sem=send_sem.at[d],
            recv_sem=recv_sem.at[d],
            device_id={"stn": to},
            device_id_type=MESH,
        )

    def arrange(order, carry):
        b = lax.rem(order + 1 + me // per_lane, stations // per_lane)
        row = lax.broadcasted_iota(jnp.int32, (LANES, columns), 0) + b * LANES
        picked = (row == target).astype(jnp.bfloat16)
        block = lax.dot_general(
            spectra[...], picked, (((1,), (1,)), ((), ())), preferred_element_type=jnp.float32
        )
        for r in range(per_lane):
            for quad in range(frames // per_lane):
                joined = jnp.zeros((inputs, LANES), jnp.float32)
                for t in range(per_lane):
                    first = (quad * per_lane + t) * inputs
                    piece = block[first : first + inputs, :]
                    if t != r:
                        piece = pltpu.roll(piece, ((t - r) * group_width) % LANES, 1)
                    joined = jnp.where(slot == t, piece, joined)
                outgoing[b * per_lane + r, :, quad * LANES : (quad + 1) * LANES] = joined.astype(
                    jnp.bfloat16
                )
        for r in range(per_lane):
            to = b * per_lane + r

            @pl.when(to != me)
            def _():
                turn_copy(lax.rem(to - me + stations, stations)).start()

        return carry

    lax.fori_loop(0, stations // per_lane, arrange, 0)

    received[me] = outgoing[me]

    def arrive(d, carry):
        turn_copy(d).wait_recv()
        return carry

    lax.fori_loop(1, stations, arrive, 0)

    total_inputs = stations * inputs
    length = frames * group_width
    per_block = ROW_BLOCK // inputs
    plane = lax.broadcasted_iota(jnp.int32, (ROW_BLOCK, length), 1) // per_group % 2
    everything = received[...].reshape(total_inputs, length)

    def correlate(b, carry):
        left = received[pl.ds(b * per_block, per_block)].reshape(ROW_BLOCK, length)
        full = left.astype(jnp.float32)
        turned = jnp.where(
            plane == 0, pltpu.roll(full, length - per_group, 1), -pltpu.roll(full, per_group, 1)
        ).astype(jnp.bfloat16)
        pair = jnp.concatenate([left, turned], axis=0)
        product = lax.dot_general(
            pair, everything, (((1,), (1,)), ((), ())), preferred_element_type=jnp.float32
        )
        products[b] = product.reshape(2, ROW_BLOCK, total_inputs)
        return carry

    blocks = out_ref.shape[0]
    last = pltpu.make_async_remote_copy(
        src_ref=products.at[pl.ds((1 - half) * blocks, blocks)],
        dst_ref=other,
        send_sem=final_sem.at[0],
        recv_sem=final_sem.at[1],
        device_id={"tim": 1 - half},
        device_id_type=MESH,
    )
    lax.fori_loop((1 - half) * blocks, (2 - half) * blocks, correlate, 0)
    last.start()
    lax.fori_loop(half * blocks, (1 + half) * blocks, correlate, 0)

    def sent(d, carry):
        turn_copy(d).wait_send()
        return carry

    lax.fori_loop(1, stations, sent, 0)

    @pl.when(half == 0)
    def _():
        near.wait_send()
        for j in range(half_steps):
            give(j).wait_send()

    last.wait()
    normaliser = 1.0 / (per_group * frames * 2)
    out_ref[...] = (products[pl.ds(half * blocks, blocks)] + other[...]) * normaliser


def arrange_planes(blocks_ref, out_ref):
    blocks, planes, rows, _ = blocks_ref.shape
    for b in range(blocks):
        for p in range(planes):
            out_ref[b * rows : (b + 1) * rows, p, :] = blocks_ref[b, p]


def per_device(samples, taps, flags, group_owner):
    inputs, frames, fft_len = samples.shape
    taps_count = taps.shape[0]
    stations = lax.axis_size("stn")
    band = flags.shape[0]
    per_group = band // stations
    columns = 2 * band
    total_inputs = stations * inputs
    blocks = total_inputs // ROW_BLOCK
    length = frames * 2 * per_group
    steps = fft_len // STEP_WIDTH
    chunks = STEP_WIDTH // LANES
    own_rows = frames * inputs
    scratch = [
        pltpu.VMEM((steps + steps // 2, inputs, frames, STEP_WIDTH), jnp.bfloat16),
        pltpu.VMEM((taps_count, fft_len), jnp.float32),
        pltpu.VMEM((fft_len // 2, columns), jnp.bfloat16),
        pltpu.VMEM((flags.shape[1], band), jnp.int32),
        pltpu.VMEM((own_rows // LANES, own_rows, LANES), jnp.bfloat16),
        pltpu.VMEM((chunks, own_rows, LANES), jnp.bfloat16),
        pltpu.VMEM((chunks, own_rows, LANES), jnp.bfloat16),
        pltpu.VMEM((2, own_rows, columns), jnp.float32),
        pltpu.VMEM((own_rows, columns), jnp.float32),
        pltpu.VMEM((frames, columns), jnp.float32),
        pltpu.VMEM((own_rows, columns), jnp.bfloat16),
        pltpu.VMEM((stations, inputs, length), jnp.bfloat16),
        pltpu.VMEM((stations, inputs, length), jnp.bfloat16),
        pltpu.VMEM((blocks, 2, ROW_BLOCK, total_inputs), jnp.float32),
        pltpu.VMEM((blocks // 2, 2, ROW_BLOCK, total_inputs), jnp.float32),
        pltpu.SemaphoreType.DMA((steps,)),
        pltpu.SemaphoreType.DMA((steps,)),
        pltpu.SemaphoreType.DMA((steps // 2,)),
        pltpu.SemaphoreType.DMA((1,)),
        pltpu.SemaphoreType.DMA((steps // 2,)),
        pltpu.SemaphoreType.DMA((steps // 2,)),
        pltpu.SemaphoreType.DMA((2,)),
        pltpu.SemaphoreType.DMA((stations,)),
        pltpu.SemaphoreType.DMA((stations,)),
        pltpu.SemaphoreType.DMA((2,)),
    ]
    shape = (blocks // 2, 2, ROW_BLOCK, total_inputs)
    kept = pltpu.VMEM if math.prod(shape) * 4 <= KEPT_LIMIT else jax.ShapeDtypeStruct
    table = jnp.asarray(table_constant(fft_len, stations, per_group))
    hbm = pl.BlockSpec(memory_space=pltpu.HBM)
    result = pl.pallas_call(
        functools.partial(kernel, (stations, per_group)),
        in_specs=[pl.BlockSpec(memory_space=pltpu.SMEM), hbm, hbm, hbm, hbm],
        out_specs=pl.BlockSpec(memory_space=pltpu.VMEM),
        out_shape=kept(shape, jnp.float32),
        scratch_shapes=scratch,
        compiler_params=pltpu.CompilerParams(
            collective_id=0, has_side_effects=True, vmem_limit_bytes=60 << 20
        ),
        name="correlator",
    )(group_owner, samples, taps, table, flags.T)
    ordered = pl.pallas_call(
        arrange_planes,
        in_specs=[pl.BlockSpec(memory_space=pltpu.VMEM)],
        out_specs=pl.BlockSpec(memory_space=pltpu.VMEM),
        out_shape=jax.ShapeDtypeStruct((total_inputs // 2, 2, total_inputs), jnp.float32),
        compiler_params=pltpu.CompilerParams(vmem_limit_bytes=result.size * 8 + (2 << 20)),
        name="planes",
    )(result)
    return ordered[None]


def solution(mesh):
    in_specs = (P(("grp", "stn"), "tim", None), P(), P("grp", None), P("grp"))
    out_specs = P(("grp", "stn"), "tim", None, None)
    return jax.shard_map(
        per_device, mesh=mesh, in_specs=in_specs, out_specs=out_specs, check_vma=False
    )
```

```python
import functools
import math

import jax
import jax.numpy as jnp
import numpy as np
from jax import lax
from jax.experimental import pallas as pl
from jax.experimental.pallas import tpu as pltpu
from jax.sharding import PartitionSpec as P

BAND_START = 1536
MESH = pl.DeviceIdType.MESH
LANES = 128
ROW_BLOCK = 64
STEP_WIDTH = 512
DEPTH = 256
GROUP = 4
KEPT_LIMIT = 1 << 20


def half_table(fft_len, channels):
    bins = np.arange(channels, dtype=np.int64) + BAND_START
    index = (np.arange(fft_len // 2, dtype=np.int64)[:, None] * bins[None]) % fft_len
    angle = index * (2.0 * math.pi / fft_len)
    amplitude = 1.0 / math.sqrt(fft_len)
    return np.cos(angle) * amplitude, -np.sin(angle) * amplitude


def table_constant(fft_len, groups, per_group):
    planes = [p.reshape(-1, groups, 1, per_group) for p in half_table(fft_len, groups * per_group)]
    stacked = np.concatenate(planes, axis=2)
    return stacked.reshape(stacked.shape[0], -1).astype(np.float32).astype(jnp.bfloat16)


def tree_sum(weights, frame, pairs):
    if len(pairs) == 1:
        return weights[pairs[0][0]] * frame[pairs[0][1]]
    middle = 1 << ((len(pairs) - 1).bit_length() - 1)
    return tree_sum(weights, frame, pairs[:middle]) + tree_sum(weights, frame, pairs[middle:])


def kernel(
    dims, owner_ref, samples_ref, taps_ref, table_ref, flags_ref, out_ref,
    wide, taps, table, flags, perm, turned, rows_b, totals, earlier,
    valid, spectra, outgoing, received, products, other,
    load_sem, taps_sem, table_sem, flags_sem, give_sem, take_sem, near_sem, send_sem, recv_sem, final_sem,
):
    stations, per_group = dims
    inputs, frames, fft_len = samples_ref.shape
    taps_count = taps_ref.shape[0]
    carry_rows = (taps_count - 1) * inputs
    own_rows = frames * inputs
    group_width = 2 * per_group
    columns = stations * group_width
    per_lane = LANES // group_width
    steps = fft_len // STEP_WIDTH
    half_steps = steps // 2
    chunks = STEP_WIDTH // LANES
    me = lax.axis_index("stn")
    half = lax.axis_index("tim")
    barrier = pltpu.get_barrier_semaphore()

    def stretch(j, base=0):
        return pl.ds(pl.multiple_of(base + j * STEP_WIDTH, STEP_WIDTH), STEP_WIDTH)

    def load(j):
        return pltpu.make_async_copy(
            samples_ref.at[:, :, stretch(j)], wide.at[j], load_sem.at[j]
        )

    def load_taps(j):
        return pltpu.make_async_copy(taps_ref.at[:, stretch(j)], taps.at[:, stretch(j)], taps_sem.at[j])

    def load_table(j):
        return pltpu.make_async_copy(table_ref.at[stretch(j)], table.at[stretch(j)], table_sem.at[j])

    load_flags = pltpu.make_async_copy(flags_ref, flags, flags_sem.at[0])

    def give(j):
        return pltpu.make_async_remote_copy(
            src_ref=samples_ref.at[:, :, stretch(j, fft_len // 2)],
            dst_ref=wide.at[steps + j],
            send_sem=give_sem.at[j],
            recv_sem=take_sem.at[j],
            device_id={"tim": 1 - half},
            device_id_type=MESH,
        )

    for j in range(half_steps):
        load(j).start()
        load_taps(j).start()
        load_table(j).start()
    load_flags.start()
    pl.semaphore_signal(barrier, inc=1, device_id={"tim": 1 - half}, device_id_type=MESH)

    def greet(d, carry):
        pl.semaphore_signal(
            barrier, inc=1, device_id={"stn": lax.rem(me + d, stations)}, device_id_type=MESH
        )
        return carry

    lax.fori_loop(1, stations, greet, 0)

    from_row = lax.broadcasted_iota(jnp.int32, (own_rows, own_rows), 0)
    from_column = lax.broadcasted_iota(jnp.int32, (own_rows, own_rows), 1)
    moving = (from_column == from_row % inputs * frames + from_row // inputs).astype(perm.dtype)
    for p in range(own_rows // LANES):
        perm[p] = moving[:, p * LANES : (p + 1) * LANES]

    pair_lanes = DEPTH // LANES
    pairs = chunks // pair_lanes

    def turn(offset, p):
        moving = jnp.concatenate([perm[q] for q in range(own_rows // LANES)], axis=1)
        block = wide[lax.div(offset, STEP_WIDTH), :, :, p * DEPTH : (p + 1) * DEPTH].reshape(own_rows, DEPTH)
        moved = jnp.dot(moving, block, preferred_element_type=jnp.float32).astype(jnp.bfloat16)
        for q in range(pair_lanes):
            turned[p * pair_lanes + q] = moved[:, q * LANES : (q + 1) * LANES]

    def filter_rows(j, base, into, outputs, p):
        blocks = []
        for c in range(p * pair_lanes, (p + 1) * pair_lanes):
            lanes = pl.ds(pl.multiple_of(base + j * STEP_WIDTH + c * LANES, LANES), LANES)
            weights = [
                jnp.broadcast_to(taps[k : k + 1, lanes], (inputs, LANES)).astype(jnp.bfloat16)
                for k in range(taps_count)
            ]
            frame = [turned[c, s * inputs : (s + 1) * inputs, :] for s in range(frames)]
            made = []
            for t in outputs:
                first = t - (taps_count - 1)
                pairs_of = [(k, first + k) for k in range(taps_count) if 0 <= first + k < frames]
                made.append(tree_sum(weights, frame, pairs_of))
            if into is not None:
                for place, value in enumerate(made):
                    into[c, place * inputs : (place + 1) * inputs, :] = value
            blocks.append(jnp.concatenate(made, axis=0))
        return blocks

    def transform(blocks, j, which, scale=None):
        stacked = jnp.concatenate(blocks, axis=1)
        high = stacked.shape[0]
        if columns <= DEPTH:
            totals[which, :high] = add(totals[which, :high], scale, stacked, table[stretch(j), :])
        else:

            def block(b, carry):
                to = pl.ds(pl.multiple_of(b * DEPTH, DEPTH), DEPTH)
                part = None if scale is None else scale[:, :DEPTH]
                totals[which, :high, to] = add(totals[which, :high, to], part, stacked, table[stretch(j), to])
                return carry

            lax.fori_loop(0, columns // DEPTH, block, 0)

    def held():
        return [rows_b[c] for c in range(chunks)]

    def add(before, scale, left, right):
        product = jnp.dot(left, right, preferred_element_type=jnp.float32)
        return before + product if scale is None else before * scale + product

    sign_row = lax.broadcasted_iota(jnp.int32, (1, columns), 1)
    bins = BAND_START + sign_row // group_width * per_group + sign_row % per_group
    sign = (1 - 2 * (bins % 2)).astype(jnp.float32)

    def sweep(count, trips, base, taps_base, outputs, total, other_total, follow, ready, flip, opening):
        def group(i, carry):
            ready(i)
            for e in range(GROUP):
                now = GROUP * i + e
                after = base + (now + 1) * STEP_WIDTH
                if e + 1 == GROUP:
                    after = jnp.where(now + 1 < count, after, follow)
                blocks = []
                for p in range(pairs):
                    blocks += filter_rows(now, taps_base, rows_b if e + 1 == GROUP else None, outputs, p)
                    turn(after, p)
                if e == 0:
                    before = jnp.where(
                        jnp.logical_and(opening, i == 0), 0, lax.rem(now + half_steps - 1, half_steps)
                    )
                    transform(held(), before, jnp.where(i == 0, other_total, total))
                if e + 1 < GROUP:
                    scale = jnp.where(now == half_steps, sign, 1.0) if flip and half_steps % GROUP == e else None
                    transform(blocks, lax.rem(now, half_steps), total, scale)
            return carry

        lax.fori_loop(0, trips, group, 0)

    def arrived(i):
        for e in range(GROUP):
            load_taps(GROUP * i + e).wait()

            @pl.when(GROUP * i + e + 1 < steps)
            def _():
                load(GROUP * i + e + 1).wait()

            @pl.when(i < half_steps // GROUP)
            def _():
                load_table(GROUP * i + e).wait()

    near = pltpu.make_async_remote_copy(
        src_ref=totals.at[1],
        dst_ref=earlier,
        send_sem=near_sem.at[0],
        recv_sem=near_sem.at[1],
        device_id={"tim": 1 - half},
        device_id_type=MESH,
    )
    own_outputs = range(frames)
    carry_outputs = range(frames, frames + taps_count - 1)
    totals[...] = jnp.zeros_like(totals)
    rows_b[...] = jnp.zeros_like(rows_b)
    load(0).wait()
    for p in range(pairs):
        turn(0, p)

    @pl.when(half == 0)
    def _():
        pl.semaphore_wait(barrier, stations)
        for j in range(half_steps):
            give(j).start()

    for j in range(half_steps, steps):
        load(j).start()
        load_taps(j).start()

    def own_ready(i):
        @pl.when(jnp.logical_or(half == 1, i >= half_steps // GROUP))
        def _():
            arrived(i)

        @pl.when(jnp.logical_and(half == 0, i == 1))
        def _():
            near.start()

        @pl.when(jnp.logical_and(half == 1, i == steps // GROUP - 1))
        def _():
            give(0).wait_recv()

    def carry_ready(i):
        @pl.when(half == 0)
        def _():
            arrived(i)

        @pl.when(half == 1)
        def _():
            for e in range(GROUP):

                @pl.when(GROUP * i + e + 1 < half_steps)
                def _():
                    give(GROUP * i + e + 1).wait_recv()

    def phase(p, carry):
        carrying = jnp.where(half == p, half_steps // GROUP, 0)
        owning = jnp.where(p == 0, steps // GROUP, 0)
        sweep(
            half_steps, carrying, half * fft_len, half * (fft_len // 2), carry_outputs,
            1, 1 - half, 0, carry_ready, False, half == 0,
        )
        sweep(steps, owning, 0, 0, own_outputs, 0, 1 - half, half * fft_len, own_ready, True, half == 1)
        return carry

    lax.fori_loop(0, 2, phase, 0)
    transform(held(), half_steps - 1, half)

    @pl.when(half == 1)
    def _():
        pl.semaphore_wait(barrier, stations)

    load_flags.wait()
    band = stations * per_group
    channel = lax.broadcasted_iota(jnp.int32, (band, columns), 0)
    column = lax.broadcasted_iota(jnp.int32, (band, columns), 1)
    spread = (channel == column // group_width * per_group + column % per_group).astype(jnp.bfloat16)
    flag_rows = flags[...].astype(jnp.float32).astype(jnp.bfloat16)
    both = jnp.dot(flag_rows, spread, preferred_element_type=jnp.float32)
    valid[...] = jnp.where(half == 0, both[:frames], both[frames:])

    lane = lax.broadcasted_iota(jnp.int32, (8, columns), 1)
    target = lane % group_width
    for g in range(stations):
        target = jnp.where(lane // group_width == g, target + owner_ref[g] * group_width, target)
    target = target[:1]
    mask = valid[...].astype(jnp.bfloat16)

    def weigh(values, low, high):
        count = high - low
        shaped = values.astype(jnp.bfloat16).reshape(count, inputs, columns)
        spectra[low * inputs : high * inputs, :] = (shaped * mask[low:high, None, :]).reshape(
            count * inputs, columns
        )

    @pl.when(half == 0)
    def _():
        weigh(totals[0] * sign, 0, frames)

    @pl.when(half == 1)
    def _():
        near.wait_recv()
        carried = carry_rows // inputs
        weigh((totals[0, :carry_rows, :] + totals[1, :carry_rows, :]) * sign + earlier[:carry_rows, :], 0, carried)
        weigh(totals[0, carry_rows:, :] * sign, carried, frames)

    slot = lax.broadcasted_iota(jnp.int32, (inputs, LANES), 1) // group_width

    def turn_copy(d):
        to = lax.rem(me + d, stations)
        return pltpu.make_async_remote_copy(
            src_ref=outgoing.at[to],
            dst_ref=received.at[me],
            send_sem=send_sem.at[d],
            recv_sem=recv_sem.at[d],
            device_id={"stn": to},
            device_id_type=MESH,
        )

    def arrange(order, carry):
        b = lax.rem(order + 1 + me // per_lane, stations // per_lane)
        row = lax.broadcasted_iota(jnp.int32, (LANES, columns), 0) + b * LANES
        picked = (row == target).astype(jnp.bfloat16)
        block = lax.dot_general(
            spectra[...], picked, (((1,), (1,)), ((), ())), preferred_element_type=jnp.float32
        )
        for r in range(per_lane):
            for quad in range(frames // per_lane):
                joined = jnp.zeros((inputs, LANES), jnp.float32)
                for t in range(per_lane):
                    first = (quad * per_lane + t) * inputs
                    piece = block[first : first + inputs, :]
                    if t != r:
                        piece = pltpu.roll(piece, ((t - r) * group_width) % LANES, 1)
                    joined = jnp.where(slot == t, piece, joined)
                outgoing[b * per_lane + r, :, quad * LANES : (quad + 1) * LANES] = joined.astype(
                    jnp.bfloat16
                )
        for r in range(per_lane):
            to = b * per_lane + r

            @pl.when(to != me)
            def _():
                turn_copy(lax.rem(to - me + stations, stations)).start()

        return carry

    lax.fori_loop(0, stations // per_lane, arrange, 0)

    received[me] = outgoing[me]

    def arrive(d, carry):
        turn_copy(d).wait_recv()
        return carry

    lax.fori_loop(1, stations, arrive, 0)

    total_inputs = stations * inputs
    length = frames * group_width
    per_block = ROW_BLOCK // inputs
    plane = lax.broadcasted_iota(jnp.int32, (ROW_BLOCK, length), 1) // per_group % 2
    everything = received[...].reshape(total_inputs, length)

    def correlate(b, carry):
        left = received[pl.ds(b * per_block, per_block)].reshape(ROW_BLOCK, length)
        full = left.astype(jnp.float32)
        turned = jnp.where(
            plane == 0, pltpu.roll(full, length - per_group, 1), -pltpu.roll(full, per_group, 1)
        ).astype(jnp.bfloat16)
        pair = jnp.concatenate([left, turned], axis=0)
        product = lax.dot_general(
            pair, everything, (((1,), (1,)), ((), ())), preferred_element_type=jnp.float32
        )
        products[b] = product.reshape(2, ROW_BLOCK, total_inputs)
        return carry

    blocks = out_ref.shape[0]
    last = pltpu.make_async_remote_copy(
        src_ref=products.at[pl.ds((1 - half) * blocks, blocks)],
        dst_ref=other,
        send_sem=final_sem.at[0],
        recv_sem=final_sem.at[1],
        device_id={"tim": 1 - half},
        device_id_type=MESH,
    )
    lax.fori_loop((1 - half) * blocks, (2 - half) * blocks, correlate, 0)
    last.start()
    lax.fori_loop(half * blocks, (1 + half) * blocks, correlate, 0)

    def sent(d, carry):
        turn_copy(d).wait_send()
        return carry

    lax.fori_loop(1, stations, sent, 0)

    @pl.when(half == 0)
    def _():
        near.wait_send()
        for j in range(half_steps):
            give(j).wait_send()

    last.wait()
    normaliser = 1.0 / (per_group * frames * 2)
    out_ref[...] = (products[pl.ds(half * blocks, blocks)] + other[...]) * normaliser


def arrange_planes(blocks_ref, out_ref):
    blocks, planes, rows, _ = blocks_ref.shape
    for b in range(blocks):
        for p in range(planes):
            out_ref[b * rows : (b + 1) * rows, p, :] = blocks_ref[b, p]


def per_device(samples, taps, flags, group_owner):
    inputs, frames, fft_len = samples.shape
    taps_count = taps.shape[0]
    stations = lax.axis_size("stn")
    band = flags.shape[0]
    per_group = band // stations
    columns = 2 * band
    total_inputs = stations * inputs
    blocks = total_inputs // ROW_BLOCK
    length = frames * 2 * per_group
    steps = fft_len // STEP_WIDTH
    chunks = STEP_WIDTH // LANES
    own_rows = frames * inputs
    scratch = [
        pltpu.VMEM((steps + steps // 2, inputs, frames, STEP_WIDTH), jnp.bfloat16),
        pltpu.VMEM((taps_count, fft_len), jnp.float32),
        pltpu.VMEM((fft_len // 2, columns), jnp.bfloat16),
        pltpu.VMEM((flags.shape[1], band), jnp.int32),
        pltpu.VMEM((own_rows // LANES, own_rows, LANES), jnp.bfloat16),
        pltpu.VMEM((chunks, own_rows, LANES), jnp.bfloat16),
        pltpu.VMEM((chunks, own_rows, LANES), jnp.bfloat16),
        pltpu.VMEM((2, own_rows, columns), jnp.float32),
        pltpu.VMEM((own_rows, columns), jnp.float32),
        pltpu.VMEM((frames, columns), jnp.float32),
        pltpu.VMEM((own_rows, columns), jnp.bfloat16),
        pltpu.VMEM((stations, inputs, length), jnp.bfloat16),
        pltpu.VMEM((stations, inputs, length), jnp.bfloat16),
        pltpu.VMEM((blocks, 2, ROW_BLOCK, total_inputs), jnp.float32),
        pltpu.VMEM((blocks // 2, 2, ROW_BLOCK, total_inputs), jnp.float32),
        pltpu.SemaphoreType.DMA((steps,)),
        pltpu.SemaphoreType.DMA((steps,)),
        pltpu.SemaphoreType.DMA((steps // 2,)),
        pltpu.SemaphoreType.DMA((1,)),
        pltpu.SemaphoreType.DMA((steps // 2,)),
        pltpu.SemaphoreType.DMA((steps // 2,)),
        pltpu.SemaphoreType.DMA((2,)),
        pltpu.SemaphoreType.DMA((stations,)),
        pltpu.SemaphoreType.DMA((stations,)),
        pltpu.SemaphoreType.DMA((2,)),
    ]
    shape = (blocks // 2, 2, ROW_BLOCK, total_inputs)
    kept = pltpu.VMEM if math.prod(shape) * 4 <= KEPT_LIMIT else jax.ShapeDtypeStruct
    table = jnp.asarray(table_constant(fft_len, stations, per_group))
    hbm = pl.BlockSpec(memory_space=pltpu.HBM)
    result = pl.pallas_call(
        functools.partial(kernel, (stations, per_group)),
        in_specs=[pl.BlockSpec(memory_space=pltpu.SMEM), hbm, hbm, hbm, hbm],
        out_specs=pl.BlockSpec(memory_space=pltpu.VMEM),
        out_shape=kept(shape, jnp.float32),
        scratch_shapes=scratch,
        compiler_params=pltpu.CompilerParams(
            collective_id=0, has_side_effects=True, vmem_limit_bytes=60 << 20
        ),
        name="correlator",
    )(group_owner, samples, taps, table, flags.T)
    ordered = pl.pallas_call(
        arrange_planes,
        in_specs=[pl.BlockSpec(memory_space=pltpu.VMEM)],
        out_specs=pl.BlockSpec(memory_space=pltpu.VMEM),
        out_shape=jax.ShapeDtypeStruct((total_inputs // 2, 2, total_inputs), jnp.float32),
        compiler_params=pltpu.CompilerParams(vmem_limit_bytes=result.size * 8 + (2 << 20)),
        name="planes",
    )(result)
    return ordered[None]


def solution(mesh):
    in_specs = (P(("grp", "stn"), "tim", None), P(), P("grp", None), P("grp"))
    out_specs = P(("grp", "stn"), "tim", None, None)
    return jax.shard_map(
        per_device, mesh=mesh, in_specs=in_specs, out_specs=out_specs, check_vma=False
    )
```
